32 devices in a mesh: batch: 8 (over z, core), seq: 4 (over y, x).
Axes of the slice: x: 2, y: 2, z: 4, core: 2. Of those that a mesh axis runs over, the one named last changes fastest.
Arguments:
- tokens: bfloat16 [8, 1024, 768], P('batch', 'seq'), may hold values from -6 to 6
- cotangent: bfloat16 [8, 1024, 768], P('batch', 'seq'), may hold values from -6 to 6
- w_query: bfloat16 [768, 768], replicated, may hold values from -0.21875 to 0.21875
- b_query: float32 [768], replicated, may hold values from -5 to 5
- w_key: bfloat16 [768, 768], replicated, may hold values from -0.21875 to 0.21875
- w_value: bfloat16 [768, 768], replicated, may hold values from -0.21875 to 0.21875
- b_value: float32 [768], replicated, may hold values from -3 to 3
- w_out: bfloat16 [768, 768], replicated, may hold values from -1.75 to 1.75
- b_out: float32 [768], replicated, may hold values from -3 to 3
- first_gain: float32 [768], replicated, may hold values from 0.1 to 1.9
- first_shift: float32 [768], replicated, may hold values from -3 to 3
- w_inner: bfloat16 [768, 3072], replicated, may hold values from -0.21875 to 0.21875
- b_inner: float32 [3072], replicated, may hold values from -3 to 3
- w_outer: bfloat16 [3072, 768], replicated, may hold values from -0.109375 to 0.109375
- b_outer: float32 [768], replicated, may hold values from -3 to 3
- second_gain: float32 [768], replicated, may hold values from 0.1 to 1.9
- second_shift: float32 [768], replicated, may hold values from -3 to 3
- global_counts: int32 [8], P('batch'), may hold values from 2 to 4
- random_blocks: int32 [8, 16, 12, 3], P('batch', 'seq'), may hold values from 0 to 15, as said below
Outputs:
- layer_out: bfloat16 [8, 1024, 768], P('batch', 'seq')
- token_grad: float32 [8, 1024, 768], P('batch', 'seq')
- grad_w_query: float32 [768, 768], replicated
- grad_b_query: float32 [768], replicated
- grad_w_key: float32 [768, 768], replicated
- grad_w_value: float32 [768, 768], replicated
- grad_b_value: float32 [768], replicated
- grad_w_out: float32 [768, 768], replicated
- grad_b_out: float32 [768], replicated
- grad_first_gain: float32 [768], replicated
- grad_first_shift: float32 [768], replicated
- grad_w_inner: float32 [768, 3072], replicated
- grad_b_inner: float32 [3072], replicated
- grad_w_outer: float32 [3072, 768], replicated
- grad_b_outer: float32 [768], replicated
- grad_second_gain: float32 [768], replicated
- grad_second_shift: float32 [768], replicated
The draws below stay inside these ranges and needn't reach their ends.
Inputs may be any that keep to these rules, and one draw needn't show every extreme that they name: `random_blocks`: in each sequence, the 144 entries of the query blocks 4 * i to 4 * i + 3 name blocks of each range 4 * j to 4 * j + 3 exactly 36 times.
All inputs are finite; a program needn't handle non-finite values.
Results may differ from the reference program's by a relative error of at most 0.015.
Values may be sent and summed in bfloat16 or wider, within the bound.
No kernel may reach another device: no remote copies, remote signals or barrier semaphores. Data moves between devices by JAX's collectives and lax.ppermute only.
A program may use at most 384 MiB of HBM per device.

```python
import math
from functools import partial
import jax
import jax.numpy as jnp
from jax import lax

D = 768
HEADS = 12
HD = 64
FF = 3072
BLK = 64
RAND = 3
GMAX = 4
BLK_DEV = 4
SEQUENCES = 8
NBLK = 16
LENGTH = 1024


def draw_random_blocks(key, part):
    shard_count = NBLK // BLK_DEV
    slot_count = BLK_DEV * HEADS * RAND
    share_size = slot_count // shard_count
    order_key, local_key = jax.random.split(jax.random.fold_in(key, 7))
    shard_keys = jax.random.split(order_key, SEQUENCES * shard_count)

    def shuffle_one(one_key):
        return jax.random.permutation(one_key, slot_count)
    orders = jax.vmap(shuffle_one)(shard_keys)
    owners = (orders // share_size).reshape(SEQUENCES, shard_count, BLK_DEV, HEADS, RAND)
    local_ids = jax.random.randint(local_key, (SEQUENCES, shard_count, BLK_DEV, HEADS, RAND), 0, BLK_DEV)
    return (owners * BLK_DEV + local_ids).reshape(SEQUENCES, NBLK, HEADS, RAND).astype(jnp.int32)


def with_ends(array, rng, least, top_value):
    spot = [jax.random.randint(jax.random.fold_in(rng, axis), (), 0, length) for axis, length in enumerate(array.shape)]
    main_axis = array.shape.index(max(array.shape))
    neighbour = spot[:main_axis] + [(spot[main_axis] + 1) % array.shape[main_axis]] + spot[main_axis + 1:]
    return array.at[tuple(spot)].set(least).at[tuple(neighbour)].set(top_value)


def shard_levels(own_key, dims, pieces, smallest, high):
    loudness, own = 1.0, jax.random.fold_in(own_key, 6)
    for dim, shards_of in pieces:
        steps = jnp.exp(jax.random.uniform(jax.random.fold_in(own, dim), (shards_of,), jnp.float32, smallest / len(pieces), high / len(pieces)))
        loudness = loudness * jnp.repeat(steps, dims[dim] // shards_of).reshape([-1 if axis == dim else 1 for axis in range(len(dims))])
    return loudness


def normal_values(own_key, shape, spread, limit, cuts=(), kind=jnp.bfloat16):
    array = jax.random.normal(own_key, shape, jnp.float32) * spread
    if len(cuts) > 0:
        array = shard_levels(own_key, shape, cuts, -0.22, 0.18) * array
    return jnp.clip(array, min=-limit, max=limit).astype(kind)


def setup_inputs(seed: int = 0) -> dict:
    seeds = jax.random.split(jax.random.key(seed), 20)
    tokens = normal_values(seeds[0], (SEQUENCES, LENGTH, D), 1.0, 6.0, ((0, 8), (1, 4)))
    cotangent = normal_values(seeds[1], (SEQUENCES, LENGTH, D), 1.0, 6.0, ((0, 8), (1, 4)))
    w_query = normal_values(seeds[2], (D, D), D ** -0.5, 0.21875)
    b_query = normal_values(seeds[3], (D,), 1.0, 5.0, (), jnp.float32)
    w_key = normal_values(seeds[4], (D, D), D ** -0.5, 0.21875)
    w_value = normal_values(seeds[5], (D, D), D ** -0.5, 0.21875)
    b_value = normal_values(seeds[6], (D,), 0.5, 3.0, (), jnp.float32)
    w_out = normal_values(seeds[7], (D, D), (D // 64) ** -0.5, 1.75)
    b_out = normal_values(seeds[8], (D,), 0.5, 3.0, (), jnp.float32)
    first_gain = jnp.clip(1.0 + 0.18 * jax.random.normal(seeds[9], (D,), jnp.float32), 0.1, 1.9)
    first_shift = normal_values(seeds[10], (D,), 0.5, 3.0, (), jnp.float32)
    w_inner = normal_values(seeds[11], (D, FF), D ** -0.5, 0.21875)
    b_inner = normal_values(seeds[12], (FF,), 0.5, 3.0, (), jnp.float32)
    w_outer = normal_values(seeds[13], (FF, D), FF ** -0.5, 0.109375)
    b_outer = normal_values(seeds[14], (D,), 0.5, 3.0, (), jnp.float32)
    second_gain = jnp.clip(1.0 + 0.18 * jax.random.normal(seeds[15], (D,), jnp.float32), 0.1, 1.9)
    second_shift = normal_values(seeds[16], (D,), 0.5, 3.0, (), jnp.float32)
    global_counts = with_ends(jax.random.randint(seeds[17], (SEQUENCES,), 2, GMAX + 1), jax.random.fold_in(seeds[17], 1), 2, GMAX).astype(jnp.int32)
    random_blocks = draw_random_blocks(jax.random.fold_in(seeds[19], 71), 0)
    return {"tokens": tokens, "cotangent": cotangent, "w_query": w_query, "b_query": b_query, "w_key": w_key, "w_value": w_value, "b_value": b_value, "w_out": w_out, "b_out": b_out, "first_gain": first_gain, "first_shift": first_shift, "w_inner": w_inner, "b_inner": b_inner, "w_outer": w_outer, "b_outer": b_outer, "second_gain": second_gain, "second_shift": second_shift, "global_counts": global_counts, "random_blocks": random_blocks}


@jax.custom_vjp
def low(v):
    return lax.optimization_barrier(v.astype(jnp.bfloat16)).astype(jnp.float32)

@jax.custom_vjp
def low_back(v):
    return v

def low_keep(v):
    return (low(v), None)

def low_pass(kept, grad):
    return (grad,)

def back_keep(v):
    return (v, None)

def back_low(kept, grad):
    return (low(grad),)
low.defvjp(low_keep, low_pass)
low_back.defvjp(back_keep, back_low)
HIGHEST = lax.Precision.HIGHEST
EPSILON = 1e-06
NEGATIVE = -1e+30

def round_both(value):
    return low(low_back(value))

def layer_norm(values, norm_gain, norm_shift):
    average = lax.optimization_barrier(jnp.mean(values, axis=-1, keepdims=True))
    centred = values - average
    variance = lax.optimization_barrier(jnp.mean(centred * centred, axis=-1, keepdims=True))
    return centred * lax.rsqrt(variance + EPSILON) * norm_gain + norm_shift

def gelu_tanh(values):
    inner_arg = 0.7978845608028654 * (values + 0.044715 * values * values * values)
    return 0.5 * values * (1.0 + jnp.tanh(inner_arg))

def softmax_rows(scores):
    row_top = lax.optimization_barrier(jnp.max(scores, axis=-1, keepdims=True))
    raised = jnp.exp(scores - row_top)
    return raised / lax.optimization_barrier(jnp.sum(raised, axis=-1, keepdims=True))

def head_attention(inputs, counts):
    head_queries, head_keys, head_values, head_picks = inputs
    length = head_queries.shape[0]
    block_count = length // BLK
    score_scale = 1.0 / math.sqrt(HD)
    query_blocks = head_queries.reshape(block_count, BLK, HD)
    key_blocks = head_keys.reshape(block_count, BLK, HD)
    value_blocks = head_values.reshape(block_count, BLK, HD)
    position = jnp.arange(block_count, dtype=jnp.int32)
    window = position[:, None] + jnp.arange(-1, 2, dtype=jnp.int32)[None, :]
    window_ok = (window >= 0) & (window < block_count)
    window = jnp.clip(window, 0, block_count - 1)
    global_ids = jnp.broadcast_to(jnp.arange(GMAX, dtype=jnp.int32)[None, :], (block_count, GMAX))
    global_ok = global_ids < counts
    chosen = jnp.concatenate([window, head_picks.astype(jnp.int32), global_ids], axis=1)
    allowed = jnp.concatenate([window_ok, jnp.ones((block_count, RAND), dtype=jnp.bool_), global_ok], axis=1)
    key_tiles = jnp.take(key_blocks, chosen, axis=0).reshape(block_count, -1, HD)
    value_tiles = jnp.take(value_blocks, chosen, axis=0).reshape(block_count, -1, HD)
    scores = low_back(jnp.einsum('nqd,nkd->nqk', query_blocks, key_tiles, precision=HIGHEST) * score_scale)
    key_mask = jnp.repeat(allowed, BLK, axis=1)[:, None, :]
    weights = low(softmax_rows(jnp.where(key_mask, scores, NEGATIVE)))
    sparse_out = jnp.einsum('nqk,nkd->nqd', weights, value_tiles, precision=HIGHEST)
    global_queries = head_queries[:GMAX * BLK]
    global_scores = low_back(jnp.dot(global_queries, head_keys.T, precision=HIGHEST) * score_scale)
    global_weights = low(softmax_rows(global_scores))
    global_out = jnp.dot(global_weights, head_values, precision=HIGHEST).reshape(GMAX, BLK, HD)
    is_global = (jnp.arange(GMAX, dtype=jnp.int32) < counts)[:, None, None]
    head_top = jnp.where(is_global, global_out, sparse_out[:GMAX])
    return jnp.concatenate([head_top, sparse_out[GMAX:]], axis=0).reshape(length, HD)

def sequence_layer(token_rows, params, counts, seq_picks):
    w_query, b_query, w_key, w_value, b_value, w_out, b_out, first_gain, first_shift, w_inner, b_inner, w_outer, b_outer, second_gain, second_shift = params
    length = token_rows.shape[0]
    queries = round_both(jnp.dot(token_rows, w_query, precision=HIGHEST) + b_query)
    key_rows = round_both(jnp.dot(token_rows, w_key, precision=HIGHEST))
    value_rows = round_both(jnp.dot(token_rows, w_value, precision=HIGHEST) + b_value)

    def split_heads(value):
        return value.reshape(length, HEADS, HD).transpose(1, 0, 2)
    per_head = lax.map(jax.checkpoint(partial(head_attention, counts=counts)), (split_heads(queries), split_heads(key_rows), split_heads(value_rows), seq_picks.transpose(1, 0, 2)))
    attended = round_both(per_head.transpose(1, 0, 2).reshape(length, D))
    branch = low_back(jnp.dot(attended, w_out, precision=HIGHEST) + b_out)
    first_norm = layer_norm(token_rows + branch, first_gain, first_shift)
    inner_pre = low_back(jnp.dot(low(first_norm), w_inner, precision=HIGHEST) + b_inner)
    outer_out = low_back(jnp.dot(low(gelu_tanh(inner_pre)), w_outer, precision=HIGHEST) + b_outer)
    return layer_norm(first_norm + outer_out, second_gain, second_shift)

def reference(tokens, cotangent, w_query, b_query, w_key, w_value, b_value, w_out, b_out, first_gain, first_shift, w_inner, b_inner, w_outer, b_outer, second_gain, second_shift, global_counts, random_blocks):
    params = tuple((item.astype(jnp.float32) for item in (w_query, b_query, w_key, w_value, b_value, w_out, b_out, first_gain, first_shift, w_inner, b_inner, w_outer, b_outer, second_gain, second_shift)))
    all_tokens = tokens.astype(jnp.float32)
    all_cotangents = cotangent.astype(jnp.float32)

    def one_sequence(totals, inputs):
        seq_tokens, seq_cot, seq_count, seq_picks = inputs

        def forward(token_rows, weights_all):
            return sequence_layer(token_rows, weights_all, seq_count, seq_picks)
        output, pullback = jax.vjp(forward, seq_tokens, params)
        token_grad, param_grads = pullback(seq_cot)
        totals = tuple((total_item + grad_item for total_item, grad_item in zip(totals, param_grads)))
        return (totals, (output.astype(jnp.bfloat16), token_grad))
    zero_grads = tuple((jnp.zeros_like(item) for item in params))
    totals, outputs = lax.scan(one_sequence, zero_grads, (all_tokens, all_cotangents, global_counts, random_blocks))
    return (outputs[0], outputs[1], totals[0], totals[1], totals[2], totals[3], totals[4], totals[5], totals[6], totals[7], totals[8], totals[9], totals[10], totals[11], totals[12], totals[13], totals[14])
```

```python
import functools
import math

import jax
import jax.numpy as jnp
from jax import lax
from jax.experimental import pallas as pl
from jax.experimental.pallas import tpu as pltpu
from jax.sharding import PartitionSpec as P

HEADS = 12
HD = 64
BLK = 64
GMAX = 4
QUAD = 4
EPSILON = 1e-06
NEGATIVE = -1e30
BF = jnp.bfloat16
F32 = jnp.float32
VMEM_BYTES = 56 * 1024 * 1024
PIECES = 16

NN = (((1,), (0,)), ((), ()))
NT = (((1,), (1,)), ((), ()))
TN = (((0,), (0,)), ((), ()))


def mm(a, b, dims=NN):
    return lax.dot_general(a, b, dims, preferred_element_type=F32)


def params(**kw):
    return pltpu.CompilerParams(vmem_limit_bytes=VMEM_BYTES, **kw)


def whole(shape):
    return pl.BlockSpec(shape, lambda *_: (0,) * len(shape))


def half_mask(values, side):
    lane = lax.broadcasted_iota(jnp.int32, values.shape, 1)
    keep = lane < HD if side == 0 else lane >= HD
    return jnp.where(keep, values, jnp.zeros_like(values))


def attend_body(rows, *refs):
    n = len(rows)
    pieces = refs[:n]
    wq, bq, wk, wv, bv, bias = refs[n : n + 6]
    q_out, k_out, v_out, o_out, lse_out = refs[n + 6 : n + 11]
    vt, sc, ot = refs[n + 11 :]
    q = (mm(pieces[0][...], wq[...]) + bq[...]).astype(BF)
    q_out[...] = (q.astype(F32) * (1.0 / math.sqrt(HD))).astype(BF)
    start = 0
    for piece, count in zip(pieces, rows):
        x = piece[...]
        k_out[start : start + count, :] = mm(x, wk[...]).astype(BF)
        v = mm(x, wv[...]) + bv[...]
        v_out[start : start + count, :] = v.astype(BF)
        vt[:, start : start + count] = v.T.astype(BF)
        start += count
    total = start
    step = 256
    per = step // BLK
    for head in range(QUAD):
        lanes = slice(head // 2 * 128, head // 2 * 128 + 128)
        qh = half_mask(q_out[:, lanes], head % 2)
        top = jnp.full((1, qh.shape[0]), NEGATIVE, F32)
        for c in range(total // step):
            part = mm(k_out[c * step : (c + 1) * step, lanes], qh, NT)
            for b in range(per):
                row = bias[head, c * per + b : c * per + b + 1, :]
                s = part[b * BLK : (b + 1) * BLK, :] + row
                sc[c * step + b * BLK : c * step + (b + 1) * BLK, :] = s
                top = jnp.maximum(top, jnp.max(s, axis=0, keepdims=True))
        acc = jnp.zeros((HD, qh.shape[0]), F32)
        norm = jnp.zeros((1, qh.shape[0]), F32)
        for c in range(total // step):
            e = jnp.exp(sc[c * step : (c + 1) * step, :] - top)
            norm = norm + jnp.sum(e, axis=0, keepdims=True)
            acc = acc + mm(vt[head * HD : (head + 1) * HD, c * step : (c + 1) * step], e.astype(BF))
        ot[head * HD : (head + 1) * HD, :] = acc / norm
        lse_out[0, head : head + 1, :] = top + jnp.log(norm)
    o_out[...] = ot[...].T


def attend(pieces, wq, bq, wk, wv, bv, bias):
    rows = tuple(p.shape[0] for p in pieces)
    total = sum(rows)
    tok, width = pieces[0].shape
    groups = HEADS // QUAD
    cols = QUAD * HD
    col = lambda r: pl.BlockSpec((r, cols), lambda g: (0, g))
    return pl.pallas_call(
        functools.partial(attend_body, rows),
        grid=(groups,),
        in_specs=[whole((r, width)) for r in rows]
        + [col(width), col(1), col(width), col(width), col(1)]
        + [pl.BlockSpec((QUAD,) + bias.shape[1:], lambda g: (g, 0, 0))],
        out_specs=[
            col(tok),
            col(total),
            col(total),
            col(tok),
            pl.BlockSpec((1, QUAD, tok), lambda g: (g, 0, 0)),
        ],
        out_shape=[
            jax.ShapeDtypeStruct((tok, width), BF),
            jax.ShapeDtypeStruct((total, width), BF),
            jax.ShapeDtypeStruct((total, width), BF),
            jax.ShapeDtypeStruct((tok, width), F32),
            jax.ShapeDtypeStruct((groups, QUAD, tok), F32),
        ],
        scratch_shapes=[
            pltpu.VMEM((cols, total), BF),
            pltpu.VMEM((total, tok), F32),
            pltpu.VMEM((cols, tok), F32),
        ],
        compiler_params=params(),
        name="attend",
    )(*pieces, wq, bq, wk, wv, bv, bias)


def norm_stats(values):
    mean = jnp.mean(values, axis=-1, keepdims=True)
    centred = values - mean
    r = lax.rsqrt(jnp.mean(centred * centred, axis=-1, keepdims=True) + EPSILON)
    return centred * r, r


def norm_back(e, u, r):
    return r * (e - jnp.mean(e, axis=-1, keepdims=True) - u * jnp.mean(e * u, axis=-1, keepdims=True))


def colsum(values):
    return jnp.sum(values, axis=0, keepdims=True)


def put_pieces(dst, base, block, mix):
    size = block.shape[0] // PIECES
    for p in range(PIECES):
        at = pl.multiple_of(base + (p ^ mix) * size, 16)
        dst[pl.ds(at, size), :] = block[p * size : (p + 1) * size, :]


def feed_body(
    info, o_in, x_in, cot_in, wo_any, wi_any, wu_any, b_out, fg, fs, b_inner, b_outer, sg, ss,
    layer_out, g_sum_out, g_att_out, dots_out, small_out, wo_grad, *rest,
):
    outer = rest[:4]
    inner = rest[4:8]
    wo, wi, wu, sems, hid_t, slope, g_in, low_t = rest[8:]
    copies = [
        pltpu.make_async_copy(src, dst, sems.at[i])
        for i, (src, dst) in enumerate(((wo_any, wo), (wi_any, wi), (wu_any, wu)))
    ]
    for c in copies:
        c.start()
    core, mix_a, mix_b = info[0], info[1], info[2]
    small_out[...] = jnp.zeros_like(small_out)
    width = wo.shape[0]
    chunks = wi.shape[1] // width
    att = o_in[...].astype(BF)
    copies[0].wait()
    first_in = x_in[...].astype(F32) + (mm(att, wo[...]) + b_out[...])
    u1, r1 = norm_stats(first_in)
    first = u1 * fg[...] + fs[...]
    low = first.astype(BF)
    copies[1].wait()
    copies[2].wait()
    out = jnp.zeros_like(first)
    for j in range(chunks):
        cols = slice(j * width, (j + 1) * width)
        v = mm(low, wi[:, cols]) + b_inner[:, cols]
        t = jnp.tanh(0.7978845608028654 * (v + 0.044715 * v * v * v))
        h = (0.5 * v * (1.0 + t))
        slope[:, cols] = 0.5 * (1.0 + t) + 0.5 * v * (1.0 - t * t) * (
            0.7978845608028654 * (1.0 + 3.0 * 0.044715 * v * v)
        )
        out = out + mm(h.astype(BF), wu[cols, :])
        put_pieces(hid_t, (j ^ (core * 2)) * width, h.T.astype(BF), mix_b if j % 2 else mix_a)
    u2, r2 = norm_stats(first + (out + b_outer[...]))
    layer_out[...] = (u2 * sg[...] + ss[...]).astype(BF)
    cot = cot_in[...].astype(F32)
    small_out[4:5, :] = colsum(cot * u2)
    small_out[5:6, :] = colsum(cot)
    g_second = norm_back(cot * sg[...], u2, r2)
    g_outer = g_second.astype(BF)
    small_out[3:4, :] = colsum(g_outer.astype(F32))
    for j in range(chunks):
        outer[j][...] = mm(hid_t[j * width : (j + 1) * width, :], g_outer).astype(BF)
    back = jnp.zeros_like(first)
    for j in range(chunks):
        cols = slice(j * width, (j + 1) * width)
        gi = (mm(g_outer, wu[cols, :], NT) * slope[:, cols]).astype(BF)
        g_in[:, cols] = gi
        small_out[6 + j : 7 + j, :] = colsum(gi.astype(F32))
        back = back + mm(gi, wi[:, cols], NT)
    flat_t = first.T.astype(BF)
    put_pieces(low_t, 0, flat_t, mix_a)
    put_pieces(low_t, width, flat_t, mix_b)
    for j in range(chunks):
        at = pl.multiple_of((j ^ (core * 2)) * width, 128)
        lhs = low_t[(j % 2) * width : (j % 2 + 1) * width, :]
        inner[j][...] = mm(lhs, g_in[:, pl.ds(at, width)]).astype(BF)
    g_first = g_second + back
    small_out[1:2, :] = colsum(g_first * u1)
    small_out[2:3, :] = colsum(g_first)
    g_sum = norm_back(g_first * fg[...], u1, r1)
    g_sum_out[...] = g_sum
    g_branch = g_sum.astype(BF)
    small_out[0:1, :] = colsum(g_branch.astype(F32))
    o = o_in[...]
    put_pieces(hid_t, 0, o.T.astype(BF), mix_a)
    wo_grad[...] = mm(hid_t[:width, :], g_branch).astype(BF)
    g_att = mm(g_branch, wo[...], NT).astype(BF)
    g_att_out[...] = g_att
    head = lax.broadcasted_iota(jnp.int32, (16, width), 0)
    lane = lax.broadcasted_iota(jnp.int32, (16, width), 1)
    pick = jnp.where(lane // HD == head, 1.0, 0.0).astype(F32)
    dots_out[...] = lax.dot_general(
        pick, g_att.astype(F32) * o, NT, precision=lax.Precision.HIGHEST, preferred_element_type=F32
    )


def feed(info, o, x, cot, wo, wi, wu, b_out, fg, fs, b_inner, b_outer, sg, ss):
    tok, width = x.shape
    ff = wi.shape[1]
    vm = pl.BlockSpec(memory_space=pltpu.VMEM)
    anyspec = pl.BlockSpec(memory_space=pl.ANY)
    sq = jax.ShapeDtypeStruct((width, width), BF)
    return pl.pallas_call(
        feed_body,
        in_specs=[pl.BlockSpec(memory_space=pltpu.SMEM), vm, vm, vm, anyspec, anyspec, anyspec] + [vm] * 7,
        out_specs=[vm] * 14,
        out_shape=[
            jax.ShapeDtypeStruct((tok, width), BF),
            jax.ShapeDtypeStruct((tok, width), F32),
            jax.ShapeDtypeStruct((tok, width), BF),
            jax.ShapeDtypeStruct((16, tok), F32),
            jax.ShapeDtypeStruct((16, width), F32),
        ]
        + [sq] * 9,
        scratch_shapes=[
            pltpu.VMEM((width, width), BF),
            pltpu.VMEM((width, ff), BF),
            pltpu.VMEM((ff, width), BF),
            pltpu.SemaphoreType.DMA((3,)),
            pltpu.VMEM((ff, tok), BF),
            pltpu.VMEM((tok, ff), F32),
            pltpu.VMEM((tok, ff), BF),
            pltpu.VMEM((2 * width, tok), BF),
        ],
        compiler_params=params(),
        name="feed",
    )(info, o, x, cot, wo, wi, wu, b_out, fg, fs, b_inner, b_outer, sg, ss)


def attend_back_body(q_in, k_in, v_in, g_in, bias, lse, dots, dq_out, dk_out, dv_out, kt, dqt):
    total = k_in.shape[0]
    step = 256
    per = step // BLK
    kt[...] = k_in[...].astype(F32).T.astype(BF)
    for pair in range(QUAD // 2):
        lanes = slice(pair * 128, pair * 128 + 128)
        qs = [half_mask(q_in[:, lanes], s) for s in range(2)]
        gs = [half_mask(g_in[:, lanes], s) for s in range(2)]
        dqs = [jnp.zeros((HD, q_in.shape[0]), F32) for _ in range(2)]
        for c in range(total // step):
            rows = slice(c * step, (c + 1) * step)
            kc = k_in[rows, lanes]
            vc = v_in[rows, lanes]
            dk = jnp.zeros((step, 128), F32)
            dv = jnp.zeros((step, 128), F32)
            for s in range(2):
                head = pair * 2 + s
                sc = mm(kc, qs[s], NT)
                dp = mm(vc, gs[s], NT)
                shift = bias[head, c * per : (c + 1) * per, :] - lse[0, head : head + 1, :]
                p = jnp.concatenate(
                    [jnp.exp(sc[b * BLK : (b + 1) * BLK, :] + shift[b : b + 1, :]) for b in range(per)], axis=0
                )
                ds = (p * (dp - dots[0, head : head + 1, :])).astype(BF)
                dv = dv + mm(p.astype(BF), gs[s])
                dk = dk + mm(ds, qs[s])
                dqs[s] = dqs[s] + mm(kt[head * HD : (head + 1) * HD, rows], ds)
            dk_out[rows, lanes] = dk.astype(BF)
            dv_out[rows, lanes] = dv.astype(BF)
        for s in range(2):
            head = pair * 2 + s
            dqt[head * HD : (head + 1) * HD, :] = dqs[s]
    dq_out[...] = (dqt[...].T * (1.0 / math.sqrt(HD))).astype(BF)


def attend_back(q, k, v, g, bias, lse, dots):
    tok, width = q.shape
    total = k.shape[0]
    groups = HEADS // QUAD
    cols = QUAD * HD
    col = lambda r: pl.BlockSpec((r, cols), lambda g: (0, g))
    stat = pl.BlockSpec((1, QUAD, tok), lambda g: (g, 0, 0))
    return pl.pallas_call(
        attend_back_body,
        grid=(groups,),
        in_specs=[col(tok), col(total), col(total), col(tok), pl.BlockSpec((QUAD,) + bias.shape[1:], lambda g: (g, 0, 0)), stat, stat],
        out_specs=[col(tok), col(total), col(total)],
        out_shape=[
            jax.ShapeDtypeStruct((tok, width), BF),
            jax.ShapeDtypeStruct((total, width), BF),
            jax.ShapeDtypeStruct((total, width), BF),
        ],
        scratch_shapes=[pltpu.VMEM((cols, total), BF), pltpu.VMEM((cols, tok), F32)],
        compiler_params=params(),
        name="attend_back",
    )(q, k, v, g, bias, lse, dots)


def weights_body(rows, info, dq, dk, dv, wo_grad, *refs):
    n = len(rows)
    pieces = refs[:n]
    keep_a, keep_b, send_a, send_b, small = refs[n : n + 5]
    xt_a, xt_b, tmp = refs[n + 5 :]
    core, mix_a, mix_b = info[0], info[1], info[2]

    @pl.when(pl.program_id(0) == 0)
    def _():
        start = 0
        for piece, count in zip(pieces, rows):
            t = piece[...].astype(F32).T.astype(BF)
            size = t.shape[0] // PIECES
            for p in range(PIECES):
                at_a = pl.multiple_of((p ^ mix_a) * size, 16)
                at_b = pl.multiple_of((p ^ mix_b) * size, 16)
                xt_a[pl.ds(at_a, size), start : start + count] = t[p * size : (p + 1) * size, :]
                xt_b[pl.ds(at_b, size), start : start + count] = t[p * size : (p + 1) * size, :]
            start += count

    own = rows[0]
    small[...] = jnp.zeros_like(small)
    small[0:1, :] = colsum(dq[...].astype(F32))
    small[1:2, :] = colsum(dv[...].astype(F32))
    tmp[0] = mm(xt_b[:, :own], dq[...]).astype(BF)
    tmp[1] = mm(xt_a[...], dk[...]).astype(BF)
    tmp[2] = mm(xt_b[...], dv[...]).astype(BF)

    @pl.when(core == 0)
    def _():
        keep_a[...] = wo_grad[...]
        keep_b[...] = tmp[0]
        send_a[...] = tmp[1]
        send_b[...] = tmp[2]

    @pl.when(core != 0)
    def _():
        send_a[...] = wo_grad[...]
        send_b[...] = tmp[0]
        keep_a[...] = tmp[1]
        keep_b[...] = tmp[2]


def weights(info, dq, dk, dv, wo_grad, pieces):
    rows = tuple(p.shape[0] for p in pieces)
    total = sum(rows)
    tok, width = dq.shape
    cols = 256
    col = lambda r: pl.BlockSpec((r, cols), lambda g: (0, g))
    sq = jax.ShapeDtypeStruct((width, width), BF)
    return pl.pallas_call(
        functools.partial(weights_body, rows),
        grid=(width // cols,),
        in_specs=[pl.BlockSpec(memory_space=pltpu.SMEM), col(tok), col(total), col(total), col(width)]
        + [whole((r, width)) for r in rows],
        out_specs=[col(width)] * 4 + [col(8)],
        out_shape=[sq] * 4 + [jax.ShapeDtypeStruct((8, width), F32)],
        scratch_shapes=[
            pltpu.VMEM((width, total), BF),
            pltpu.VMEM((width, total), BF),
            pltpu.VMEM((3, width, cols), BF),
        ],
        compiler_params=params(),
        name="weights",
    )(info, dq, dk, dv, wo_grad, *pieces)


def token_body(rows, dq, dk, dv, wq, wk, wv, g_sum, *refs):
    n = len(rows)
    own_out = refs[0]
    outs = refs[1:n]
    start = 0
    for i, count in enumerate(rows):
        t = mm(dk[start : start + count, :], wk[...], NT) + mm(dv[start : start + count, :], wv[...], NT)
        if i == 0:
            own_out[...] = t + mm(dq[...], wq[...], NT) + g_sum[...]
        else:
            outs[i - 1][...] = t.astype(BF)
        start += count


def token_parts(rows, dq, dk, dv, wq, wk, wv, g_sum):
    tok, width = dq.shape
    vm = pl.BlockSpec(memory_space=pltpu.VMEM)
    return pl.pallas_call(
        functools.partial(token_body, rows),
        in_specs=[vm] * 7,
        out_specs=[vm] * len(rows),
        out_shape=[jax.ShapeDtypeStruct((tok, width), F32)]
        + [jax.ShapeDtypeStruct((r, width), BF) for r in rows[1:]],
        compiler_params=params(),
        name="token_parts",
    )(dq, dk, dv, wq, wk, wv, g_sum)


def unpack_body(kind, layout, info, *refs):
    n = len(layout)
    ins = refs[:n]
    outs = refs[n:]
    core = info[0]
    for ref, (rc, stream, first) in zip(ins, layout):
        mix = info[1 + stream]
        piece = PIECE_ROWS
        for i in range(ref.shape[0] // piece):
            p = (first + i) ^ mix
            block = ref[i * piece : (i + 1) * piece, :].astype(F32)
            at = p * piece
            chunk = ((rc ^ core) * 2) + stream
            width = ref.shape[1]
            if kind == "rows":
                outs[0][pl.ds(pl.multiple_of(chunk * width + at, 8), piece), :] = block
            elif kind == "cols":
                outs[0][pl.ds(pl.multiple_of(at, 8), piece), pl.ds(pl.multiple_of(chunk * width, 128), width)] = block
            else:
                for c in range(2):

                    @pl.when(core == c)
                    def _():
                        outs[(rc ^ c) * 2 + stream][pl.ds(pl.multiple_of(at, 8), piece), :] = block


PIECE_ROWS = 768 // PIECES


def unpack(kind, info, arrays, layout, width, ff):
    vm = pl.BlockSpec(memory_space=pltpu.VMEM)
    shapes = {
        "rows": [(ff, width)],
        "cols": [(width, ff)],
        "four": [(width, width)] * 4,
    }[kind]
    return pl.pallas_call(
        functools.partial(unpack_body, kind, layout),
        in_specs=[pl.BlockSpec(memory_space=pltpu.SMEM)] + [vm] * len(arrays),
        out_specs=[vm] * len(shapes),
        out_shape=[jax.ShapeDtypeStruct(s, F32) for s in shapes],
        compiler_params=params(),
        name="unpack_" + kind,
    )(info, *arrays)


def xor_permute(value, axis, mask):
    size = lax.axis_size(axis)
    return lax.ppermute(value, axis, [(i, i ^ mask) for i in range(size)])


def plus(a, b):
    return (a.astype(F32) + b.astype(F32)).astype(BF)


def reduce_stream(keep, send, bits):
    run = plus(keep, xor_permute(send, "batch", 1))
    for mask in bits:
        half = run.shape[0] // 2
        got = xor_permute(run[half:], "seq", mask)
        run = plus(run[:half], got)
    depth = lax.axis_size("batch") // 2
    piece = run.shape[0] // depth
    own = run[:piece].astype(F32)
    for k in range(1, depth):
        own = own + xor_permute(run[k * piece : (k + 1) * piece], "batch", 2 * k).astype(F32)
    return own.astype(BF)


def gather_stream(own, bits, stream):
    depth = lax.axis_size("batch") // 2
    run = jnp.concatenate([own] + [xor_permute(own, "batch", 2 * k) for k in range(1, depth)], axis=0)
    parts = [(run, 0)]
    count = depth
    for mask in reversed(bits):
        body = run if len(parts) == 1 else jnp.concatenate([a for a, _ in parts], axis=0)
        got = xor_permute(body, "seq", mask)
        parts.append((got, count))
        count *= 2
    found = []
    for array, first in parts:
        found.append((array, (0, stream, first)))
        found.append((xor_permute(array, "batch", 1), (1, stream, first)))
    return found


def sum_chunk(kind, info, keeps, sends, width, ff):
    found = []
    for stream in range(2):
        bits = (1, 2) if stream == 0 else (2, 1)
        own = reduce_stream(keeps[stream], sends[stream], bits)
        found += gather_stream(own, bits, stream)
    return unpack(kind, info, [a for a, _ in found], tuple(l for _, l in found), width, ff)


def sum_chunk_plain(kind, info, keeps, sends, width, ff):
    stacked = jnp.concatenate([keeps[0], keeps[1], sends[0], sends[1]], axis=0)
    axes = ("batch", "seq")
    part = lax.psum_scatter(stacked, axes, scatter_dimension=0, tiled=True)
    full = lax.all_gather(part, axes, axis=0, tiled=True)
    arrays = [full[i * width : (i + 1) * width] for i in range(4)]
    layout = ((0, 0, 0), (0, 1, 0), (1, 0, 0), (1, 1, 0))
    return unpack(kind, info, arrays, layout, width, ff)


def gather_tokens(x, small):
    size = lax.axis_size("seq")
    if small:
        a = xor_permute(x, "seq", 1)
        b = xor_permute(x, "seq", 2)
        half = x.shape[0] // 2
        return [x, a, b, xor_permute(a[:half], "seq", 2), xor_permute(b[half:], "seq", 1)]
    return [x] + [xor_permute(x, "seq", k) for k in range(1, size)]


def multiplicity_bias(random_blocks, count, shard_index, shard_count, blocks_dev):
    order = shard_index ^ jnp.arange(shard_count, dtype=jnp.int32)
    key_ids = (order[:, None] * blocks_dev + jnp.arange(blocks_dev, dtype=jnp.int32)[None, :]).reshape(-1)
    query_ids = shard_index * blocks_dev + jnp.arange(blocks_dev, dtype=jnp.int32)
    near = (jnp.abs(key_ids[:, None] - query_ids[None, :]) <= 1).astype(jnp.int32)
    lead = (key_ids < count).astype(jnp.int32)
    picks = random_blocks.transpose(1, 0, 2)
    times = jnp.sum((picks[:, None, :, :] == key_ids[None, :, None, None]).astype(jnp.int32), axis=-1)
    times = times + near[None] + lead[None, :, None]
    times = jnp.where((query_ids < count)[None, None, :], 1, times)
    bias = jnp.where(times > 0, jnp.log(jnp.maximum(times, 1).astype(F32)), NEGATIVE)
    return jnp.repeat(bias, BLK, axis=2)


def on_device(
    tokens, cotangent, w_query, b_query, w_key, w_value, b_value, w_out, b_out, first_gain, first_shift,
    w_inner, b_inner, w_outer, b_outer, second_gain, second_shift, global_counts, random_blocks,
):
    _, tok, width = tokens.shape
    ff = w_inner.shape[1]
    blocks_dev = tok // BLK
    shard_count = lax.axis_size("seq")
    shard = lax.axis_index("seq")
    batch = lax.axis_index("batch")
    direct = shard_count == 4 and lax.axis_size("batch") == 8
    if direct:
        x_bit, y_bit, z_bits = shard & 1, shard >> 1, batch >> 1
        info = jnp.stack(
            [batch & 1, (x_bit << 3) | (y_bit << 2) | z_bits, (y_bit << 3) | (x_bit << 2) | z_bits]
        ).astype(jnp.int32)
    else:
        info = jnp.zeros((3,), jnp.int32)
    x = tokens.reshape(tok, width)
    row = lambda v: v.reshape(1, -1)
    bias = multiplicity_bias(random_blocks[0], global_counts[0], shard, shard_count, blocks_dev)
    pieces = gather_tokens(x, direct)
    rows = tuple(p.shape[0] for p in pieces)
    q, k, v, o, lse = attend(pieces, w_query, row(b_query), w_key, w_value, row(b_value), bias)
    fed = feed(
        info, o, x, cotangent.reshape(tok, width), w_out, w_inner, w_outer, row(b_out), row(first_gain),
        row(first_shift), row(b_inner), row(b_outer), row(second_gain), row(second_shift),
    )
    layer_out, g_sum, g_att, dots, small, wo_grad = fed[:6]
    outer, inner = fed[6:10], fed[10:14]
    dots = dots[:HEADS].reshape(HEADS // QUAD, QUAD, tok)
    dq, dk, dv = attend_back(q, k, v, g_att, bias, lse, dots)
    mixed = weights(info, dq, dk, dv, wo_grad, pieces)
    parts = token_parts(rows, dq, dk, dv, w_query, w_key, w_value, g_sum)
    if direct:
        got = [xor_permute(parts[1], "seq", 1), xor_permute(parts[2], "seq", 2)]
        got.append(xor_permute(jnp.concatenate(parts[3:], axis=0), "seq", 3))
    else:
        got = [xor_permute(p, "seq", k) for k, p in enumerate(parts[1:], 1)]
    token_grad = parts[0]
    for g in got:
        token_grad = token_grad + g.astype(F32)
    total = sum_chunk if direct else sum_chunk_plain
    (d_outer,) = total("rows", info, outer[:2], outer[2:], width, ff)
    (d_inner,) = total("cols", info, inner[:2], inner[2:], width, ff)
    d_out, d_query, d_key, d_value = total("four", info, mixed[0:2], mixed[2:4], width, ff)
    vectors = lax.psum(jnp.concatenate([small, mixed[4]], axis=0), ("batch", "seq"))
    return (
        layer_out.reshape(1, tok, width),
        token_grad.reshape(1, tok, width),
        d_query,
        vectors[16],
        d_key,
        d_value,
        vectors[17],
        d_out,
        vectors[0],
        vectors[1],
        vectors[2],
        d_inner,
        vectors[6:10].reshape(-1),
        d_outer,
        vectors[3],
        vectors[4],
        vectors[5],
    )


def solution(mesh):
    token_spec = P("batch", "seq", None)
    placed = (token_spec, token_spec) + (P(),) * 15 + (P("batch"), P("batch", "seq", None, None))
    return jax.shard_map(
        on_device,
        mesh=mesh,
        in_specs=placed,
        out_specs=(token_spec, token_spec) + (P(),) * 15,
        check_vma=False,
    )
```

```python
import functools
import math

import jax
import jax.numpy as jnp
from jax import lax
from jax.experimental import pallas as pl
from jax.experimental.pallas import tpu as pltpu
from jax.sharding import PartitionSpec as P

HEADS = 12
HD = 64
BLK = 64
GMAX = 4
QUAD = 4
EPSILON = 1e-06
NEGATIVE = -1e30
BF = jnp.bfloat16
F32 = jnp.float32
VMEM_BYTES = 24 * 1024 * 1024
EVENT_FLOPS = 50 * 10**6

NN = (((1,), (0,)), ((), ()))
NT = (((1,), (1,)), ((), ()))
TN = (((0,), (0,)), ((), ()))


def mm(a, b, dims=NN):
    return lax.dot_general(a, b, dims, preferred_element_type=F32)


def params(**kw):
    return pltpu.CompilerParams(vmem_limit_bytes=VMEM_BYTES, **kw)


def cost(flops, bytes_accessed, exps=0):
    return pl.CostEstimate(flops=flops * 100, bytes_accessed=bytes_accessed * 100, transcendentals=exps * 100)


def ordered(body, order, in_specs, args, name, out_specs, out_shape, **kw):
    if order is None:
        return pl.pallas_call(
            body, in_specs=in_specs, out_specs=out_specs, out_shape=out_shape, name=name, **kw
        )(*args)
    one = not isinstance(out_shape, (list, tuple))
    specs, shapes = ([out_specs], [out_shape]) if one else (list(out_specs), list(out_shape))
    marks = [] if order.last is None else [order.last]
    n, made = len(args), len(shapes)
    mark = jax.ShapeDtypeStruct((8, 128), F32)

    def kernel(*refs):
        outs = refs[n + len(marks) :]
        outs[made][...] = jnp.zeros_like(outs[made])
        body(*refs[:n], *outs[:made], *outs[made + 1 :])

    mark_spec = pl.BlockSpec((8, 128), lambda *_: (0, 0))
    *out, order.last = pl.pallas_call(
        kernel,
        in_specs=list(in_specs) + [pl.BlockSpec(memory_space=pl.ANY)] * len(marks),
        out_specs=specs + [mark_spec],
        out_shape=shapes + [mark],
        name=name,
        **kw,
    )(*args, *marks)
    return out[0] if one else out


def whole(shape):
    return pl.BlockSpec(shape, lambda *_: (0,) * len(shape))


def half_mask(values, side):
    lane = lax.broadcasted_iota(jnp.int32, values.shape, 1)
    keep = lane < HD if side == 0 else lane >= HD
    return jnp.where(keep, values, jnp.zeros_like(values))


def attend_body(rows, *refs):
    n = len(rows)
    pieces = refs[:n]
    wq, wk, wv, vec, bias = refs[n : n + 5]
    q_out, k_out, v_out, o_out, lse_out = refs[n + 5 : n + 10]
    vt, sc, ot = refs[n + 10 :]
    q = (mm(pieces[0][...], wq[...]) + vec[0:1, :]).astype(BF)
    q_out[...] = (q.astype(F32) * (1.0 / math.sqrt(HD))).astype(BF)
    start = 0
    for piece, count in zip(pieces, rows):
        x = piece[...]
        k_out[0, start : start + count, :] = mm(x, wk[...]).astype(BF)
        v = mm(x, wv[...]) + vec[1:2, :]
        v_out[0, start : start + count, :] = v.astype(BF)
        vt[:, start : start + count] = v.T.astype(BF)
        start += count
    total = start
    step = 256
    per = step // BLK
    for head in range(QUAD):
        lanes = slice(head // 2 * 128, head // 2 * 128 + 128)
        qh = half_mask(q_out[:, lanes], head % 2)
        top = jnp.full((1, qh.shape[0]), NEGATIVE, F32)
        for c in range(total // step):
            part = mm(k_out[0, c * step : (c + 1) * step, lanes], qh, NT)
            for b in range(per):
                row = bias[head, c * per + b : c * per + b + 1, :]
                s = part[b * BLK : (b + 1) * BLK, :] + row
                sc[c * step + b * BLK : c * step + (b + 1) * BLK, :] = s
                top = jnp.maximum(top, jnp.max(s, axis=0, keepdims=True))
        acc = jnp.zeros((HD, qh.shape[0]), F32)
        norm = jnp.zeros((1, qh.shape[0]), F32)
        for c in range(total // step):
            e = jnp.exp(sc[c * step : (c + 1) * step, :] - top)
            norm = norm + jnp.sum(e, axis=0, keepdims=True)
            acc = acc + mm(vt[head * HD : (head + 1) * HD, c * step : (c + 1) * step], e.astype(BF))
        ot[head * HD : (head + 1) * HD, :] = acc / norm
        lse_out[0, head : head + 1, :] = top + jnp.log(norm)
    o_out[...] = ot[...].T


def attend(order, pieces, wq, wk, wv, vec, bias):
    rows = tuple(p.shape[0] for p in pieces)
    total = sum(rows)
    tok, width = pieces[0].shape
    groups = HEADS // QUAD
    cols = QUAD * HD
    col = lambda r: pl.BlockSpec((r, cols), lambda g: (0, g))
    return ordered(
        functools.partial(attend_body, rows),
        order,
        [whole((r, width)) for r in rows]
        + [col(width), col(width), col(width), col(vec.shape[0])]
        + [pl.BlockSpec((QUAD,) + bias.shape[1:], lambda g: (g, 0, 0))],
        (*pieces, *(pltpu.with_memory_space_constraint(w, pltpu.HBM) for w in (wq, wk, wv)), vec, bias),
        "attend",
        grid=(groups,),
        out_specs=[
            col(tok),
            pl.BlockSpec((1, total, cols), lambda g: (g, 0, 0)),
            pl.BlockSpec((1, total, cols), lambda g: (g, 0, 0)),
            col(tok),
            pl.BlockSpec((1, QUAD, tok), lambda g: (g, 0, 0)),
        ],
        out_shape=[
            pltpu.HBM((tok, width), BF),
            pltpu.HBM((groups, total, cols), BF),
            pltpu.HBM((groups, total, cols), BF),
            jax.ShapeDtypeStruct((tok, width), F32),
            jax.ShapeDtypeStruct((groups, QUAD, tok), F32),
        ],
        scratch_shapes=[
            pltpu.VMEM((cols, total), BF),
            pltpu.VMEM((total, tok), F32),
            pltpu.VMEM((cols, tok), F32),
        ],
        cost_estimate=cost(2 * total * 256 * (2 * HEADS * tok + 3 * width * 2), 4 * total * width * 2, HEADS * tok * total),
        compiler_params=params(),
    )


def norm_stats(values):
    mean = jnp.mean(values, axis=-1, keepdims=True)
    centred = values - mean
    r = lax.rsqrt(jnp.mean(centred * centred, axis=-1, keepdims=True) + EPSILON)
    return centred * r, r


def norm_back(e, u, r):
    return r * (e - jnp.mean(e, axis=-1, keepdims=True) - u * jnp.mean(e * u, axis=-1, keepdims=True))


def colsum(values):
    return jnp.sum(values, axis=0, keepdims=True)


def put_pieces(dst, base, block, mix, size=96):
    for p in range(block.shape[0] // size):
        at = pl.multiple_of(base + (p ^ mix) * size, 16)
        dst[pl.ds(at, size), :] = block[p * size : (p + 1) * size, :]


def feed_body(
    info, o_in, x_in, cot_in, wo_any, wi_any, wu_any, vec,
    layer_out, u1_out, r1_out, g_second_out, g_outer_out, slope, small_out, hid_t, send,
    wo, wi, wu, sems,
):
    copies = [
        pltpu.make_async_copy(src, dst, sems.at[i])
        for i, (src, dst) in enumerate(((wo_any, wo), (wi_any, wi), (wu_any, wu)))
    ]
    for c in copies:
        c.start()
    small_out[...] = jnp.zeros_like(small_out)
    width = wo.shape[0]
    chunks = wi.shape[1] // width
    b_out, fg, fs, b_outer, sg, ss = (vec[i : i + 1, :] for i in range(2, 8))
    att = o_in[...].astype(BF)
    copies[0].wait()
    first_in = x_in[...].astype(F32) + (mm(att, wo[...]) + b_out)
    u1, r1 = norm_stats(first_in)
    u1_out[...] = u1
    r1_out[...] = jnp.broadcast_to(r1, r1_out.shape)
    first = u1 * fg + fs
    low = first.astype(BF)
    copies[1].wait()
    copies[2].wait()
    out = jnp.zeros_like(first)
    for j in range(chunks):
        cols = slice(j * width, (j + 1) * width)
        v = mm(low, wi[:, cols]) + vec[8 + j : 9 + j, :]
        t = jnp.tanh(0.7978845608028654 * (v + 0.044715 * v * v * v))
        h = 0.5 * v * (1.0 + t)
        slope[:, cols] = 0.5 * (1.0 + t) + 0.5 * v * (1.0 - t * t) * (
            0.7978845608028654 * (1.0 + 3.0 * 0.044715 * v * v)
        )
        out = out + mm(h.astype(BF), wu[cols, :])
        put_pieces(hid_t, j * width, h.T.astype(BF), info[2 + 2 * j // chunks])
    u2, r2 = norm_stats(first + (out + b_outer))
    layer_out[...] = (u2 * sg + ss).astype(BF)
    cot = cot_in[...].astype(F32)
    small_out[4:5, :] = colsum(cot * u2)
    small_out[5:6, :] = colsum(cot)
    g_second = norm_back(cot * sg, u2, r2)
    g_second_out[...] = g_second
    g_outer = g_second.astype(BF)
    g_outer_out[...] = g_outer
    small_out[3:4, :] = colsum(g_outer.astype(F32))
    for j in range(chunks // 2):
        at = pl.multiple_of((j ^ info[1]) * width, width)
        send[j * width : (j + 1) * width, :] = mm(hid_t[pl.ds(at, width), :], g_outer).astype(BF)


VM = pl.BlockSpec(memory_space=pltpu.VMEM)
SM = pl.BlockSpec(memory_space=pltpu.SMEM)
ANYWHERE = pl.BlockSpec(memory_space=pl.ANY)


def feed(order, info, o, x, cot, wo, wi, wu, vec):
    tok, width = x.shape
    ff = wi.shape[1]
    return ordered(
        feed_body,
        order,
        [SM, VM, VM, VM, ANYWHERE, ANYWHERE, ANYWHERE, VM],
        (info, o, x, cot, wo, wi, wu, vec,),
        "feed",
        out_specs=[VM] * 9,
        out_shape=[
            jax.ShapeDtypeStruct((tok, width), BF),
            jax.ShapeDtypeStruct((tok, width), F32),
            jax.ShapeDtypeStruct((tok, 128), F32),
            jax.ShapeDtypeStruct((tok, width), F32),
            jax.ShapeDtypeStruct((tok, width), BF),
            jax.ShapeDtypeStruct((tok, ff), F32),
            jax.ShapeDtypeStruct((8, width), F32),
            jax.ShapeDtypeStruct((ff, tok), BF),
            pltpu.HBM((ff // 2, width), BF),
        ],
        scratch_shapes=[
            pltpu.VMEM((width, width), BF),
            pltpu.VMEM((width, ff), BF),
            pltpu.VMEM((ff, width), BF),
            pltpu.SemaphoreType.DMA((3,)),
        ],
        cost_estimate=cost(2 * tok * width * (5 * ff // 2 + width), 4 * (width * ff * 2), tok * ff),
        compiler_params=params(),
    )


def inner_back_body(
    info, u1_in, g_second_in, g_outer_in, slope, hid_t, wi_any, wu_any, vec,
    keep, g_in, low_t, back_out, small_out, send,
    wi, wu, sems,
):
    copies = [
        pltpu.make_async_copy(src, dst, sems.at[i]) for i, (src, dst) in enumerate(((wu_any, wu), (wi_any, wi)))
    ]
    for c in copies:
        c.start()
    small_out[...] = jnp.zeros_like(small_out)
    width = wi.shape[0]
    chunks = wi.shape[1] // width
    g_outer = g_outer_in[...]
    for j in range(chunks // 2):
        at = pl.multiple_of((j ^ info[0]) * width, width)
        keep[j * width : (j + 1) * width, :] = mm(hid_t[pl.ds(at, width), :], g_outer).astype(BF)
    flat_t = (u1_in[...] * vec[3:4, :] + vec[4:5, :]).T.astype(BF)
    for c in range(2):
        put_pieces(low_t.at[c], 0, flat_t, info[2 + c])
    back = g_second_in[...]
    copies[0].wait()
    copies[1].wait()
    for j in range(chunks):
        cols = slice(j * width, (j + 1) * width)
        gi = (mm(g_outer, wu[cols, :], NT) * slope[:, cols]).astype(BF)
        g_in[:, cols] = gi
        small_out[j : j + 1, :] = colsum(gi.astype(F32))
        back = back + mm(gi, wi[:, cols], NT)
    back_out[...] = back
    for j in range(chunks // 2):
        at = pl.multiple_of((j ^ info[1]) * width, width)
        send[j * width : (j + 1) * width, :] = mm(low_t[1 - info[4]], g_in[:, pl.ds(at, width)]).astype(BF)


def inner_back(order, info, u1, g_second, g_outer, slope, hid_t, wi, wu, vec):
    tok, width = u1.shape
    ff = wi.shape[1]
    half = pltpu.HBM((ff // 2, width), BF)
    return ordered(
        inner_back_body,
        order,
        [SM] + [VM] * 5 + [ANYWHERE] * 2 + [VM],
        (info, u1, g_second, g_outer, slope, hid_t, wi, wu, vec,),
        "inner_back",
        out_specs=[VM] * 6,
        out_shape=[
            half,
            jax.ShapeDtypeStruct((tok, ff), BF),
            jax.ShapeDtypeStruct((2, width, tok), BF),
            jax.ShapeDtypeStruct((tok, width), F32),
            jax.ShapeDtypeStruct((8, width), F32),
            half,
        ],
        scratch_shapes=[
            pltpu.VMEM((width, ff), BF),
            pltpu.VMEM((ff, width), BF),
            pltpu.SemaphoreType.DMA((2,)),
        ],
        cost_estimate=cost(2 * tok * width * 3 * ff, 4 * (width * ff * 2)),
        compiler_params=params(),
    )


def branch_back_body(
    info, o_in, u1_in, r1_in, back_in, g_in, low_t, wo_in, vec,
    keep, g_sum_out, g_att_out, dots_out, small_out, wo_a,
    att_t,
):
    small_out[...] = jnp.zeros_like(small_out)
    width = wo_in.shape[0]
    for j in range(keep.shape[0] // width):
        at = pl.multiple_of((j ^ info[0]) * width, width)
        keep[j * width : (j + 1) * width, :] = mm(low_t[info[4]], g_in[:, pl.ds(at, width)]).astype(BF)
    back, u1 = back_in[...], u1_in[...]
    small_out[1:2, :] = colsum(back * u1)
    small_out[2:3, :] = colsum(back)
    g_sum = norm_back(back * vec[3:4, :], u1, r1_in[:, 0:1])
    g_sum_out[...] = g_sum
    g_branch = g_sum.astype(BF)
    small_out[0:1, :] = colsum(g_branch.astype(F32))
    o = o_in[...]
    g_att = mm(g_branch, wo_in[...], NT).astype(BF)
    g_att_out[...] = g_att
    put_pieces(att_t, 0, o.T.astype(BF), info[2])
    wo_a[...] = mm(att_t[...], g_branch).astype(BF)
    head = lax.broadcasted_iota(jnp.int32, (16, width), 0)
    lane = lax.broadcasted_iota(jnp.int32, (16, width), 1)
    pick = jnp.where(lane // HD == head, 1.0, 0.0).astype(F32)
    dots_out[...] = lax.dot_general(
        pick, g_att.astype(F32) * o, NT, precision=lax.Precision.HIGHEST, preferred_element_type=F32
    )


def branch_back(order, info, o, u1, r1, back, g_in, low_t, wo, vec):
    tok, width = o.shape
    ff = g_in.shape[1]
    return ordered(
        branch_back_body,
        order,
        [SM] + [VM] * 8,
        (info, o, u1, r1, back, g_in, low_t, wo, vec,),
        "branch_back",
        out_specs=[VM] * 6,
        out_shape=[
            pltpu.HBM((ff // 2, width), BF),
            pltpu.HBM((tok, width), F32),
            pltpu.HBM((tok, width), BF),
            jax.ShapeDtypeStruct((16, tok), F32),
            jax.ShapeDtypeStruct((8, width), F32),
            pltpu.HBM((width, width), BF),
        ],
        scratch_shapes=[pltpu.VMEM((width, tok), BF)],
        cost_estimate=cost(2 * tok * width * (ff // 2 + 2 * width), 4 * width * ff),
        compiler_params=params(),
    )


def attend_back_body(q_in, k_in, v_in, g_in, bias, lse, dots, dq_out, dk_out, dv_out, kt, dqt):
    total = k_in.shape[1]
    step = 256
    per = step // BLK
    kt[...] = k_in[0].astype(F32).T.astype(BF)
    for pair in range(QUAD // 2):
        lanes = slice(pair * 128, pair * 128 + 128)
        qs = [half_mask(q_in[:, lanes], s) for s in range(2)]
        gs = [half_mask(g_in[:, lanes], s) for s in range(2)]
        dqs = [jnp.zeros((HD, q_in.shape[0]), F32) for _ in range(2)]
        for c in range(total // step):
            rows = slice(c * step, (c + 1) * step)
            kc = k_in[0, rows, lanes]
            vc = v_in[0, rows, lanes]
            dk = jnp.zeros((step, 128), F32)
            dv = jnp.zeros((step, 128), F32)
            for s in range(2):
                head = pair * 2 + s
                sc = mm(kc, qs[s], NT)
                dp = mm(vc, gs[s], NT)
                shift = bias[head, c * per : (c + 1) * per, :] - lse[0, head : head + 1, :]
                p = jnp.concatenate(
                    [jnp.exp(sc[b * BLK : (b + 1) * BLK, :] + shift[b : b + 1, :]) for b in range(per)], axis=0
                )
                ds = (p * (dp - dots[0, head : head + 1, :])).astype(BF)
                dv = dv + mm(p.astype(BF), gs[s])
                dk = dk + mm(ds, qs[s])
                dqs[s] = dqs[s] + mm(kt[head * HD : (head + 1) * HD, rows], ds)
            dk_out[0, rows, lanes] = dk.astype(BF)
            dv_out[0, rows, lanes] = dv.astype(BF)
        for s in range(2):
            head = pair * 2 + s
            dqt[head * HD : (head + 1) * HD, :] = dqs[s]
    dq_out[0] = (dqt[...].T * (1.0 / math.sqrt(HD))).astype(BF)


def attend_back(order, q, k, v, g, bias, lse, dots):
    tok, width = q.shape
    groups, total, cols = k.shape
    col = pl.BlockSpec((tok, cols), lambda i: (0, i))
    group = lambda r: pl.BlockSpec((1, r, cols), lambda i: (i, 0, 0))
    stat = pl.BlockSpec((1, QUAD, tok), lambda i: (i, 0, 0))
    return ordered(
        attend_back_body,
        order,
        [col, group(total), group(total), col]
        + [pl.BlockSpec((QUAD,) + bias.shape[1:], lambda i: (i, 0, 0)), stat, stat],
        (*(pltpu.with_memory_space_constraint(a, pltpu.HBM) for a in (q, k, v, g)), bias, lse, dots),
        "attend_back",
        grid=(groups,),
        out_specs=[group(tok), group(total), group(total)],
        out_shape=[jax.ShapeDtypeStruct((groups, r, cols), BF) for r in (tok, total, total)],
        scratch_shapes=[pltpu.VMEM((cols, total), BF), pltpu.VMEM((cols, tok), F32)],
        cost_estimate=cost(HEADS * 5 * 2 * tok * total * 256, 4 * total * width * 2, HEADS * tok * total),
        compiler_params=params(),
    )


def weights_body(rows, smalls, info, wo_grad, *refs):
    n = len(rows)
    small_in, refs = refs[:smalls], refs[smalls:]
    groups = HEADS // QUAD
    dqs, dks, dvs = refs[:3]
    pieces = refs[3 : 3 + n]
    keep, send = refs[3 + n : 5 + n]
    x0, x1, tmp, small = refs[5 + n :]
    own = rows[0]
    start = 0
    for piece, count in zip(pieces, rows):
        t = piece[...].astype(F32).T.astype(BF)
        for p in range(t.shape[0] // 96):
            for xt, mix in ((x0, info[2]), (x1, info[3])):
                if start < own or xt is x1:
                    at = pl.multiple_of((p ^ mix) * 96, 16)
                    xt[pl.ds(at, 96), start : start + count] = t[p * 96 : (p + 1) * 96, :]
        start += count
    small[...] = jnp.zeros_like(small)
    cols = QUAD * HD
    width = keep.shape[1]
    for g in range(groups):
        lanes = slice(g * cols, (g + 1) * cols)
        small[0:1, lanes] = colsum(dqs[g].astype(F32))
        small[1:2, lanes] = colsum(dvs[g].astype(F32))
        tmp[0] = wo_grad[:, lanes]
        tmp[1] = mm(x0[...], dqs[g]).astype(BF)
        tmp[2] = mm(x1[...], dks[g]).astype(BF)
        tmp[3] = mm(x1[...], dvs[g]).astype(BF)
        for j in range(2):
            keep[j * width : (j + 1) * width, lanes] = tmp[j ^ info[0]]
            send[j * width : (j + 1) * width, lanes] = tmp[j ^ info[1]]
    tail = jnp.concatenate([r[...] for r in small_in] + [small[...]], axis=0).astype(BF)
    keep[2 * width :, :] = tail
    send[2 * width :, :] = tail


def weights(order, info, dqs, dks, dvs, wo_grad, pieces, smalls):
    rows = tuple(p.shape[0] for p in pieces)
    total = sum(rows)
    width = wo_grad.shape[0]
    _, tok, cols = dqs.shape
    half = pltpu.HBM((2 * width + 8 * (len(smalls) + 1), width), BF)
    count = 1 + len(smalls) + 3 + len(rows)
    return ordered(
        functools.partial(weights_body, rows, len(smalls)),
        order,
        [SM] + [VM] * count,
        (info, wo_grad, *smalls, dqs, dks, dvs, *pieces),
        "weights",
        out_specs=[VM] * 2,
        out_shape=[half, half],
        scratch_shapes=[
            pltpu.VMEM((width, tok), BF),
            pltpu.VMEM((width, total), BF),
            pltpu.VMEM((4, width, cols), BF),
            pltpu.VMEM((8, width), F32),
        ],
        cost_estimate=cost(2 * width * width * (tok + 2 * total), 4 * width * width * 4),
        compiler_params=params(),
    )


def token_body(starts, count, info, wq, wk, wv, g_sum, *refs):
    groups = HEADS // QUAD
    dqs, dks, dvs = refs[:3]
    own, outs = refs[3], refs[4:]
    cols = QUAD * HD

    def part(place):
        rows = pl.ds(place * count if isinstance(place, int) else pl.multiple_of(place * count, count), count)
        t = jnp.zeros((count, wq.shape[0]), F32)
        for g in range(groups):
            lanes = slice(g * cols, (g + 1) * cols)
            t = t + mm(dks[g, rows, :], wk[:, lanes], NT)
            t = t + mm(dvs[g, rows, :], wv[:, lanes], NT)
        return t

    t = part(0) + g_sum[...]
    for g in range(groups):
        t = t + mm(dqs[g], wq[:, g * cols : (g + 1) * cols], NT)
    own[...] = t
    for out, places in zip(outs, starts):
        for i, (base, sign) in enumerate(places):
            place = base if sign == 0 else base + sign * info[4]
            out[i * count : (i + 1) * count, :] = part(place).astype(BF)


def token_parts(order, starts, info, dqs, dks, dvs, wq, wk, wv, g_sum):
    tok, width = g_sum.shape
    return ordered(
        functools.partial(token_body, starts, tok),
        order,
        [SM] + [VM] * (4 + 3),
        (info, wq, wk, wv, g_sum, dqs, dks, dvs),
        "token_parts",
        out_specs=[VM] * (1 + len(starts)),
        out_shape=[jax.ShapeDtypeStruct((tok, width), F32)]
        + [jax.ShapeDtypeStruct((tok * len(p), width), BF) for p in starts],
        cost_estimate=cost(2 * width * width * 9 * tok, 4 * width * width * 4),
        compiler_params=params(),
    )


def unpack_body(kind, blocks, made, info, *refs):
    n = len(blocks)
    ins = refs[:n]
    refs = refs[n + made :]
    count = len(refs) - 2
    outs, wide, sems = refs[:count], refs[count], refs[count + 1]
    size = 96
    width = ins[0].shape[1]
    places = []
    for b, (ref, (side, j)) in enumerate(zip(ins, blocks)):
        for i in range(width // size):
            at = pl.multiple_of((i ^ info[5 + side]) * size, 32)
            wide[b, pl.ds(at, size), :] = ref[i * size : (i + 1) * size, :].astype(F32)
        chunk = info[side] ^ j
        if kind == "four":
            places.append([(chunk == c, outs[c]) for c in range(4)])
        else:
            at = pl.multiple_of(chunk * width, width)
            places.append([(None, outs[0].at[pl.ds(at, width), :] if kind == "rows" else outs[0].at[:, pl.ds(at, width)])])
        for when, out in places[b]:
            copy = pltpu.make_async_copy(wide.at[b], out, sems.at[b])
            if when is None:
                copy.start()
            else:
                pl.when(when)(copy.start)
    for b in range(n):
        for when, out in places[b]:
            copy = pltpu.make_async_copy(wide.at[b], out, sems.at[b])
            if when is None:
                copy.wait()
            else:
                pl.when(when)(copy.wait)


def unpack(order, kind, info, arrays, blocks, width, ff, made=()):
    shapes = {
        "rows": [(ff, width)],
        "cols": [(width, ff)],
        "four": [(width, width)] * 4,
    }[kind]
    return ordered(
        functools.partial(unpack_body, kind, blocks, len(made)),
        order,
        [SM] + [VM] * len(arrays) + [ANYWHERE] * len(made),
        (info, *arrays, *made),
        "unpack_" + kind,
        out_specs=[ANYWHERE] * len(shapes),
        out_shape=[jax.ShapeDtypeStruct(s, F32) for s in shapes],
        scratch_shapes=[pltpu.VMEM((len(arrays), width, width), F32), pltpu.SemaphoreType.DMA((len(arrays),))],
        input_output_aliases={1 + len(arrays) + i: i for i in range(len(made))},
        cost_estimate=cost(ff * width, 6 * ff * width),
        compiler_params=params(),
    )


def xor_permute(value, axis, mask):
    size = lax.axis_size(axis)
    return lax.ppermute(value, axis, [(i, i ^ mask) for i in range(size)])


def rows_at(count, index):
    return pl.BlockSpec((count, 768), lambda *_: (index, 0))


def combine_body(ways, terms, extras, *refs):
    ins, outs = refs[: ways * terms + extras], refs[ways * terms + extras :]
    for w in range(ways):
        value = ins[w * terms][...].astype(F32)
        for r in ins[w * terms + 1 : (w + 1) * terms]:
            value = value + r[...].astype(F32)
        outs[w][: value.shape[0], :] = value.astype(BF)
    if extras:
        tail = (ins[ways * terms][...].astype(F32) + ins[ways * terms + 1][...].astype(F32)).astype(BF)
        for out in outs:
            out[out.shape[0] - tail.shape[0] :, :] = tail


def combine(order, count, ways, extras=()):
    width = ways[0][0][0].shape[1]
    terms = [t for way in ways for t in way]
    made = jax.ShapeDtypeStruct((count + (32 if extras else 0), width), BF)
    return ordered(
        functools.partial(combine_body, len(ways), len(ways[0]), len(extras)),
        order,
        [rows_at(count, i) for _, i in terms] + [rows_at(32, i) for _, i in extras],
        (*(a for a, _ in terms), *(a for a, _ in extras)),
        "combine",
        grid=(1,),
        out_specs=[pl.BlockSpec(made.shape, lambda *_: (0, 0))] * len(ways),
        out_shape=[made] * len(ways),
        cost_estimate=cost(EVENT_FLOPS, 1 << 20),
        compiler_params=params(),
    )


def finish_body(parts, extras, *refs):
    ins, outs = refs[: parts + extras], refs[parts + extras :]
    value = ins[0][...].astype(F32)
    for r in ins[1:parts]:
        value = value + r[...].astype(F32)
    outs[0][...] = value.astype(BF)
    if extras:
        outs[1][...] = ins[parts][...].astype(F32) + ins[parts + 1][...].astype(F32)


def finish(order, arrays, count, extras=()):
    width = arrays[0].shape[1]
    out = [jax.ShapeDtypeStruct((count, width), BF)]
    if extras:
        out.append(jax.ShapeDtypeStruct((32, width), F32))
    return ordered(
        functools.partial(finish_body, len(arrays), len(extras)),
        order,
        [rows_at(count, 0)] * len(arrays) + [rows_at(32, i) for _, i in extras],
        (*arrays, *(a for a, _ in extras)),
        "finish",
        grid=(1,),
        out_specs=[pl.BlockSpec(o.shape, lambda *_: (0, 0)) for o in out],
        out_shape=out,
        cost_estimate=cost(EVENT_FLOPS, 1 << 20),
        compiler_params=params(),
    )


def token_sum_body(own, first, second, out):
    out[...] = own[...] + (first[...].astype(F32) + second[...].astype(F32))


def token_sum(order, own, first, second):
    tok, width = own.shape
    block = pl.BlockSpec((tok, width), lambda *_: (0, 0))
    return ordered(
        token_sum_body,
        order,
        [block] * 3,
        (own, first, second),
        "token_sum",
        grid=(1,),
        out_specs=block,
        out_shape=jax.ShapeDtypeStruct((tok, width), F32),
        cost_estimate=cost(EVENT_FLOPS, 1 << 20),
        compiler_params=params(),
    )


def stack_body(*refs):
    at = 0
    for r in refs[:-1]:
        refs[-1][at : at + r.shape[0], :] = r[...]
        at += r.shape[0]


def stack(order, arrays):
    rows, width = sum(a.shape[0] for a in arrays), arrays[0].shape[1]
    return ordered(
        stack_body,
        order,
        [VM] * len(arrays),
        (*arrays,),
        "stack",
        out_specs=VM,
        out_shape=jax.ShapeDtypeStruct((rows, width), arrays[0].dtype),
        cost_estimate=cost(EVENT_FLOPS, 1 << 20),
        compiler_params=params(),
    )


STAGES = (((1, 0), (2, 0)), ((2, 0), (1, 0)), ((0, 2), (0, 4)), ((0, 4), (0, 2)))


def swap(value, stage):
    shards = lax.axis_size("seq")
    pairs = []
    for b in range(lax.axis_size("batch")):
        of_shard, of_batch = STAGES[stage][b % 2]
        pairs += [(b * shards + s, (b ^ of_batch) * shards + (s ^ of_shard)) for s in range(shards)]
    return lax.ppermute(value, ("batch", "seq"), pairs)


class Order:
    def __init__(self):
        self.last = None


class Unit:
    def __init__(self, order, keep, got, rows):
        self.order, self.rows, self.stage = order, rows, 0
        self.parts = [keep, got]
        self.extra = [(a, rows // 32) for a in self.parts] if keep.shape[0] > rows else []

    def step(self):
        if self.stage < 4:
            half = self.rows // 2
            (sent,) = combine(self.order, half, [[(p, 1) for p in self.parts]], self.extra)
            got = swap(sent, self.stage)
            if self.extra:
                self.extra = [(sent, half // 32), (got, half // 32)]
            self.parts.append(got)
            self.rows = half
        else:
            if self.stage == 4:
                body, *tail = finish(self.order, self.parts, self.rows, self.extra)
                self.extra = tail[0] if tail else None
            else:
                body = stack(self.order, self.held)
            self.held = [body, swap(body, 7 - self.stage)]
        self.stage += 1

    def forward(self):
        self.others = [xor_permute(a, "batch", 1) for a in self.held]


def summed_plain(info, first, second, third, tokens, width, ff):
    axes = ("batch", "seq")

    def whole_sum(keep, send):
        part = lax.psum_scatter(jnp.concatenate([keep, send], axis=0), axes, scatter_dimension=0, tiled=True)
        return lax.all_gather(part, axes, axis=0, tiled=True)

    blocks = ((0, 0), (0, 1), (1, 0), (1, 1))

    def placed(kind, pair):
        total = whole_sum(*pair)
        return unpack(None, kind, info, [total[i * width : (i + 1) * width] for i in range(4)], blocks, width, ff)

    d_outer = placed("rows", first)
    d_inner = placed("cols", second)
    d_four = placed("four", third)
    return d_outer, d_inner, d_four, [xor_permute(t, "seq", k) for k, t in enumerate(tokens, 1)]


def gather_tokens(x, small):
    size = lax.axis_size("seq")
    if small:
        a = xor_permute(x, "seq", 1)
        b = xor_permute(x, "seq", 2)
        half = x.shape[0] // 2
        return [x, a, b, xor_permute(a[:half], "seq", 2), xor_permute(b[half:], "seq", 1)]
    return [x] + [xor_permute(x, "seq", k) for k in range(1, size)]


def multiplicity_bias(random_blocks, count, shard_index, shard_count, blocks_dev):
    order = shard_index ^ jnp.arange(shard_count, dtype=jnp.int32)
    key_ids = (order[:, None] * blocks_dev + jnp.arange(blocks_dev, dtype=jnp.int32)[None, :]).reshape(-1)
    query_ids = shard_index * blocks_dev + jnp.arange(blocks_dev, dtype=jnp.int32)
    near = (jnp.abs(key_ids[:, None] - query_ids[None, :]) <= 1).astype(jnp.int32)
    lead = (key_ids < count).astype(jnp.int32)
    picks = random_blocks.transpose(1, 0, 2)
    times = jnp.sum((picks[:, None, :, :] == key_ids[None, :, None, None]).astype(jnp.int32), axis=-1)
    times = times + near[None] + lead[None, :, None]
    times = jnp.where((query_ids < count)[None, None, :], 1, times)
    bias = jnp.where(times > 0, jnp.log(jnp.maximum(times, 1).astype(F32)), NEGATIVE)
    return jnp.repeat(bias, BLK, axis=2)


def on_device(
    tokens, cotangent, w_query, b_query, w_key, w_value, b_value, w_out, b_out, first_gain, first_shift,
    w_inner, b_inner, w_outer, b_outer, second_gain, second_shift, global_counts, random_blocks,
):
    _, tok, width = tokens.shape
    ff = w_inner.shape[1]
    blocks_dev = tok // BLK
    shard_count = lax.axis_size("seq")
    shard = lax.axis_index("seq")
    batch = lax.axis_index("batch")
    direct = shard_count == 4 and lax.axis_size("batch") == 8
    if direct:
        core, z = batch & 1, batch >> 1
        x_bit, y_bit = shard & 1, shard >> 1
        first = jnp.where(core == 0, x_bit, y_bit)
        low_z, high_z = z & 1, z >> 1
        mix_0, mix_1 = y_bit * 4 + low_z * 2 + high_z, x_bit * 4 + high_z * 2 + low_z
        info = [core * 2 + first, (1 - core) * 2 + (x_bit + y_bit - first), mix_0, mix_1, core]
        info += [jnp.where(core == 0, mix_0, mix_1), jnp.where(core == 0, mix_1, mix_0)]
        info = jnp.stack(info).astype(jnp.int32)
    else:
        info = jnp.array([0, 2, 0, 0, 0, 0, 0], jnp.int32)
    x = tokens.reshape(tok, width)
    vec = jnp.concatenate(
        [b_query, b_value, b_out, first_gain, first_shift, b_outer, second_gain, second_shift, b_inner]
    ).reshape(-1, width)
    bias = multiplicity_bias(random_blocks[0], global_counts[0], shard, shard_count, blocks_dev)
    pieces = gather_tokens(x, direct)
    rows = tuple(p.shape[0] for p in pieces)
    groups = HEADS // QUAD
    order = Order() if direct else None
    pairs = ((0, 0), (0, 1), (1, 0), (1, 1))
    q, k, v, o, lse = attend(order, pieces, w_query, w_key, w_value, vec, bias)
    layer_out, u1, r1, g_second, g_outer, slope, small_1, hid_t, send_1 = feed(
        order, info, o, x, cotangent.reshape(tok, width), w_out, w_inner, w_outer, vec
    )

    def exchange(value):
        return xor_permute(value, "batch", 1) if direct else value

    got_1 = exchange(send_1)
    keep_1, g_in, low_t, back, small_2, send_2 = inner_back(
        order, info, u1, g_second, g_outer, slope, hid_t, w_inner, w_outer, vec
    )
    if direct:
        one = Unit(order, keep_1, got_1, 2 * width)
        one.step()
    keep_2, g_sum, g_att, dots, small_3, wo_grad = branch_back(order, info, o, u1, r1, back, g_in, low_t, w_out, vec)
    dots = dots[:HEADS].reshape(groups, QUAD, tok)
    got_2 = exchange(send_2)

    def attend_step():
        return attend_back(order, q, k, v, g_att, bias, lse, dots)

    def weights_step():
        return weights(order, info, *backs, wo_grad, pieces, smalls)

    def token_step(starts):
        return token_parts(order, starts, info, *backs, w_query, w_key, w_value, g_sum)

    smalls = (small_1, small_2, small_3)
    if direct:
        two = Unit(order, keep_2, got_2, 2 * width)
        two.step()
        backs = attend_step()
        one.step()
        keep_3, send_3 = weights_step()
        three = Unit(order, keep_3, exchange(send_3), 2 * width)
        two.step()
        one.step()
        parts = token_step((((1, 1), (3, 0)), ((2, -1),)))
        got_a = swap(parts[1], 0)
        two.step()
        one.step()
        three.step()
        two.step()
        one.step()
        (relay,) = combine(order, tok, [[(parts[2], 0), (got_a, 1)]])
        got_b = swap(relay, 1)
        two.step()
        one.step()
        three.step()
        token_grad = token_sum(order, parts[0], got_a, got_b)
        two.step()
        one.step()
        three.step()
        two.step()
        one.step()
        three.step()
        two.step()
        three.step()
        three.step()
        one.forward()
        (d_outer,) = unpack(order, "rows", info, one.held + one.others, pairs, width, ff)
        three.step()
        two.forward()
        (d_inner,) = unpack(order, "cols", info, two.held + two.others, pairs, width, ff)
        three.step()
        three.others = [xor_permute(three.held[0], "batch", 1)]
        made = unpack(order, "four", info, [three.held[0], three.others[0]], pairs[::2], width, ff)
        three.held[1], *made = lax.optimization_barrier((three.held[1], *made))
        three.others.append(xor_permute(three.held[1], "batch", 1))
        made = unpack(order, "four", info, [three.held[1]], pairs[1:2], width, ff, made)
        d_out, d_query, d_key, d_value = unpack(order, "four", info, [three.others[1]], pairs[3:], width, ff, made)
        vectors = three.extra
    else:
        backs = attend_step()
        keep_3, send_3 = weights_step()
        parts = token_step(tuple(((i, 0),) for i in range(1, shard_count)))
        vectors = lax.psum(keep_3[2 * width :].astype(F32), ("batch", "seq"))
        third = (keep_3[: 2 * width], send_3[: 2 * width])
        d_outer, d_inner, d_four, got = summed_plain(
            info, (keep_1, send_1), (keep_2, send_2), third, parts[1:], width, ff
        )
        (d_outer,), (d_inner,) = d_outer, d_inner
        d_out, d_query, d_key, d_value = d_four
        token_grad = sum([g.astype(F32) for g in got], parts[0])
    return (
        layer_out.reshape(1, tok, width),
        token_grad.reshape(1, tok, width),
        d_query,
        vectors[24],
        d_key,
        d_value,
        vectors[25],
        d_out,
        vectors[16],
        vectors[17],
        vectors[18],
        d_inner,
        vectors[8:12].reshape(-1),
        d_outer,
        vectors[3],
        vectors[4],
        vectors[5],
    )


def solution(mesh):
    token_spec = P("batch", "seq", None)
    placed = (token_spec, token_spec) + (P(),) * 15 + (P("batch"), P("batch", "seq", None, None))
    return jax.shard_map(
        on_device,
        mesh=mesh,
        in_specs=placed,
        out_specs=(token_spec, token_spec) + (P(),) * 15,
        check_vma=False,
    )
```

```python
import functools
import math

import jax
import jax.numpy as jnp
from jax import lax
from jax.experimental import pallas as pl
from jax.experimental.pallas import tpu as pltpu
from jax.sharding import PartitionSpec as P

HEADS = 12
HD = 64
BLK = 64
GMAX = 4
QUAD = 4
EPSILON = 1e-06
NEGATIVE = -1e30
BF = jnp.bfloat16
F32 = jnp.float32
VMEM_BYTES = 24 * 1024 * 1024
EVENT_FLOPS = 50 * 10**6
BACK_FLOPS = 5 * 10**7

NN = (((1,), (0,)), ((), ()))
NT = (((1,), (1,)), ((), ()))
TN = (((0,), (0,)), ((), ()))


def mm(a, b, dims=NN):
    return lax.dot_general(a, b, dims, preferred_element_type=F32)


def params(**kw):
    return pltpu.CompilerParams(vmem_limit_bytes=VMEM_BYTES, **kw)


def cost(flops, bytes_accessed, exps=0):
    return pl.CostEstimate(flops=flops * 100, bytes_accessed=bytes_accessed * 100, transcendentals=exps * 100)


def ordered(body, order, in_specs, args, name, out_specs, out_shape, **kw):
    if order is None:
        return pl.pallas_call(
            body, in_specs=in_specs, out_specs=out_specs, out_shape=out_shape, name=name, **kw
        )(*args)
    one = not isinstance(out_shape, (list, tuple))
    specs, shapes = ([out_specs], [out_shape]) if one else (list(out_specs), list(out_shape))
    marks = [] if order.last is None else [order.last]
    n, made = len(args), len(shapes)
    mark = jax.ShapeDtypeStruct((8, 128), F32)

    def kernel(*refs):
        outs = refs[n + len(marks) :]
        outs[made][...] = jnp.zeros_like(outs[made])
        body(*refs[:n], *outs[:made], *outs[made + 1 :])

    mark_spec = pl.BlockSpec((8, 128), lambda *_: (0, 0))
    *out, order.last = pl.pallas_call(
        kernel,
        in_specs=list(in_specs) + [pl.BlockSpec(memory_space=pl.ANY)] * len(marks),
        out_specs=specs + [mark_spec],
        out_shape=shapes + [mark],
        name=name,
        **kw,
    )(*args, *marks)
    return out[0] if one else out


def whole(shape):
    return pl.BlockSpec(shape, lambda *_: (0,) * len(shape))


def half_mask(values, side):
    lane = lax.broadcasted_iota(jnp.int32, values.shape, 1)
    keep = lane < HD if side == 0 else lane >= HD
    return jnp.where(keep, values, jnp.zeros_like(values))


def attend_body(rows, *refs):
    n = len(rows)
    pieces = refs[:n]
    wq, wk, wv, vec, bias = refs[n : n + 5]
    q_out, k_out, v_out, o_out, lse_out = refs[n + 5 : n + 10]
    vt, sc, ot = refs[n + 10 :]
    q = (mm(pieces[0][...], wq[...]) + vec[0:1, :]).astype(BF)
    q_out[...] = (q.astype(F32) * (1.0 / math.sqrt(HD))).astype(BF)
    start = 0
    for piece, count in zip(pieces, rows):
        x = piece[...]
        k_out[0, start : start + count, :] = mm(x, wk[...]).astype(BF)
        v = mm(x, wv[...]) + vec[1:2, :]
        v_out[0, start : start + count, :] = v.astype(BF)
        vt[:, start : start + count] = v.T.astype(BF)
        start += count
    total = start
    step = 256
    per = step // BLK
    for head in range(QUAD):
        lanes = slice(head // 2 * 128, head // 2 * 128 + 128)
        qh = half_mask(q_out[:, lanes], head % 2)
        top = jnp.full((1, qh.shape[0]), NEGATIVE, F32)
        for c in range(total // step):
            part = mm(k_out[0, c * step : (c + 1) * step, lanes], qh, NT)
            for b in range(per):
                row = bias[head, c * per + b : c * per + b + 1, :]
                s = part[b * BLK : (b + 1) * BLK, :] + row
                sc[c * step + b * BLK : c * step + (b + 1) * BLK, :] = s
                top = jnp.maximum(top, jnp.max(s, axis=0, keepdims=True))
        acc = jnp.zeros((HD, qh.shape[0]), F32)
        norm = jnp.zeros((1, qh.shape[0]), F32)
        for c in range(total // step):
            e = jnp.exp(sc[c * step : (c + 1) * step, :] - top)
            norm = norm + jnp.sum(e, axis=0, keepdims=True)
            acc = acc + mm(vt[head * HD : (head + 1) * HD, c * step : (c + 1) * step], e.astype(BF))
        ot[head * HD : (head + 1) * HD, :] = acc / norm
        lse_out[0, head : head + 1, :] = top + jnp.log(norm)
    o_out[...] = ot[...].T


def attend(order, pieces, wq, wk, wv, vec, bias):
    rows = tuple(p.shape[0] for p in pieces)
    total = sum(rows)
    tok, width = pieces[0].shape
    groups = HEADS // QUAD
    cols = QUAD * HD
    col = lambda r: pl.BlockSpec((r, cols), lambda g: (0, g))
    return ordered(
        functools.partial(attend_body, rows),
        order,
        [whole((r, width)) for r in rows]
        + [col(width), col(width), col(width), col(vec.shape[0])]
        + [pl.BlockSpec((QUAD,) + bias.shape[1:], lambda g: (g, 0, 0))],
        (*pieces, *(pltpu.with_memory_space_constraint(w, pltpu.HBM) for w in (wq, wk, wv)), vec, bias),
        "attend",
        grid=(groups,),
        out_specs=[
            col(tok),
            pl.BlockSpec((1, total, cols), lambda g: (g, 0, 0)),
            pl.BlockSpec((1, total, cols), lambda g: (g, 0, 0)),
            col(tok),
            pl.BlockSpec((1, QUAD, tok), lambda g: (g, 0, 0)),
        ],
        out_shape=[
            pltpu.HBM((tok, width), BF),
            pltpu.HBM((groups, total, cols), BF),
            pltpu.HBM((groups, total, cols), BF),
            jax.ShapeDtypeStruct((tok, width), F32),
            jax.ShapeDtypeStruct((groups, QUAD, tok), F32),
        ],
        scratch_shapes=[
            pltpu.VMEM((cols, total), BF),
            pltpu.VMEM((total, tok), F32),
            pltpu.VMEM((cols, tok), F32),
        ],
        cost_estimate=cost(2 * total * 256 * (2 * HEADS * tok + 3 * width * 2), 4 * total * width * 2, HEADS * tok * total),
        compiler_params=params(),
    )


def norm_stats(values):
    mean = jnp.mean(values, axis=-1, keepdims=True)
    centred = values - mean
    r = lax.rsqrt(jnp.mean(centred * centred, axis=-1, keepdims=True) + EPSILON)
    return centred * r, r


def norm_back(e, u, r):
    return r * (e - jnp.mean(e, axis=-1, keepdims=True) - u * jnp.mean(e * u, axis=-1, keepdims=True))


def colsum(values):
    return jnp.sum(values, axis=0, keepdims=True)


def put_pieces(dst, base, block, mix, size=96):
    for p in range(block.shape[0] // size):
        at = pl.multiple_of(base + (p ^ mix) * size, 16)
        dst[pl.ds(at, size), :] = block[p * size : (p + 1) * size, :]


def feed_body(
    info, o_in, x_in, cot_in, wo, wi, wu, vec,
    layer_out, u1_out, r1_out, g_second_out, g_outer_out, slope, small_out, hid_t, send,
):
    small_out[...] = jnp.zeros_like(small_out)
    width = wo.shape[0]
    chunks = wi.shape[1] // width
    b_out, fg, fs, b_outer, sg, ss = (vec[i : i + 1, :] for i in range(2, 8))
    att = o_in[...].astype(BF)
    first_in = x_in[...].astype(F32) + (mm(att, wo[...]) + b_out)
    u1, r1 = norm_stats(first_in)
    u1_out[...] = u1
    r1_out[...] = jnp.broadcast_to(r1, r1_out.shape)
    first = u1 * fg + fs
    low = first.astype(BF)
    out = jnp.zeros_like(first)
    for j in range(chunks):
        cols = slice(j * width, (j + 1) * width)
        v = mm(low, wi[:, cols]) + vec[8 + j : 9 + j, :]
        t = jnp.tanh(0.7978845608028654 * (v + 0.044715 * v * v * v))
        h = 0.5 * v * (1.0 + t)
        slope[:, cols] = 0.5 * (1.0 + t) + 0.5 * v * (1.0 - t * t) * (
            0.7978845608028654 * (1.0 + 3.0 * 0.044715 * v * v)
        )
        out = out + mm(h.astype(BF), wu[cols, :])
        put_pieces(hid_t, j * width, h.T.astype(BF), info[2 + 2 * j // chunks])
    u2, r2 = norm_stats(first + (out + b_outer))
    layer_out[...] = (u2 * sg + ss).astype(BF)
    cot = cot_in[...].astype(F32)
    small_out[4:5, :] = colsum(cot * u2)
    small_out[5:6, :] = colsum(cot)
    g_second = norm_back(cot * sg, u2, r2)
    g_second_out[...] = g_second
    g_outer = g_second.astype(BF)
    g_outer_out[...] = g_outer
    small_out[3:4, :] = colsum(g_outer.astype(F32))
    for j in range(chunks // 2):
        at = pl.multiple_of((j ^ info[1]) * width, width)
        send[j * width : (j + 1) * width, :] = mm(hid_t[pl.ds(at, width), :], g_outer).astype(BF)


VM = pl.BlockSpec(memory_space=pltpu.VMEM)
SM = pl.BlockSpec(memory_space=pltpu.SMEM)
ANYWHERE = pl.BlockSpec(memory_space=pl.ANY)


def feed(order, info, o, x, cot, wo, wi, wu, vec):
    tok, width = x.shape
    ff = wi.shape[1]
    return ordered(
        feed_body,
        order,
        [SM] + [VM] * 7,
        (info, o, x, cot, wo, wi, wu, vec,),
        "feed",
        out_specs=[VM] * 9,
        out_shape=[
            jax.ShapeDtypeStruct((tok, width), BF),
            jax.ShapeDtypeStruct((tok, width), F32),
            jax.ShapeDtypeStruct((tok, 128), F32),
            jax.ShapeDtypeStruct((tok, width), F32),
            jax.ShapeDtypeStruct((tok, width), BF),
            jax.ShapeDtypeStruct((tok, ff), F32),
            jax.ShapeDtypeStruct((8, width), F32),
            jax.ShapeDtypeStruct((ff, tok), BF),
            pltpu.HBM((ff // 2, width), BF),
        ],
        cost_estimate=cost(2 * tok * width * (5 * ff // 2 + width), 4 * (width * ff * 2), tok * ff),
        compiler_params=params(),
    )


def inner_back_body(
    info, u1_in, g_second_in, g_outer_in, slope, hid_t, wi, wu, vec,
    keep, g_in, low_t, back_out, small_out, send,
):
    small_out[...] = jnp.zeros_like(small_out)
    width = wi.shape[0]
    chunks = wi.shape[1] // width
    g_outer = g_outer_in[...]
    for j in range(chunks // 2):
        at = pl.multiple_of((j ^ info[0]) * width, width)
        keep[j * width : (j + 1) * width, :] = mm(hid_t[pl.ds(at, width), :], g_outer).astype(BF)
    flat_t = (u1_in[...] * vec[3:4, :] + vec[4:5, :]).T.astype(BF)
    for c in range(2):
        put_pieces(low_t.at[c], 0, flat_t, info[2 + c])
    back = g_second_in[...]
    for j in range(chunks):
        cols = slice(j * width, (j + 1) * width)
        gi = (mm(g_outer, wu[cols, :], NT) * slope[:, cols]).astype(BF)
        g_in[:, cols] = gi
        small_out[j : j + 1, :] = colsum(gi.astype(F32))
        back = back + mm(gi, wi[:, cols], NT)
    back_out[...] = back
    for j in range(chunks // 2):
        at = pl.multiple_of((j ^ info[1]) * width, width)
        send[j * width : (j + 1) * width, :] = mm(low_t[1 - info[4]], g_in[:, pl.ds(at, width)]).astype(BF)


def inner_back(order, info, u1, g_second, g_outer, slope, hid_t, wi, wu, vec):
    tok, width = u1.shape
    ff = wi.shape[1]
    half = pltpu.HBM((ff // 2, width), BF)
    return ordered(
        inner_back_body,
        order,
        [SM] + [VM] * 8,
        (info, u1, g_second, g_outer, slope, hid_t, wi, wu, vec,),
        "inner_back",
        out_specs=[VM] * 6,
        out_shape=[
            half,
            jax.ShapeDtypeStruct((tok, ff), BF),
            jax.ShapeDtypeStruct((2, width, tok), BF),
            jax.ShapeDtypeStruct((tok, width), F32),
            jax.ShapeDtypeStruct((8, width), F32),
            half,
        ],
        cost_estimate=cost(2 * tok * width * 3 * ff, 4 * (width * ff * 2)),
        compiler_params=params(),
    )


def branch_back_body(
    info, o_in, u1_in, r1_in, back_in, g_in, low_t, wo_in, vec,
    keep, g_sum_out, g_att_out, dots_out, small_out, wo_a,
    att_t,
):
    small_out[...] = jnp.zeros_like(small_out)
    width = wo_in.shape[0]
    for j in range(keep.shape[0] // width):
        at = pl.multiple_of((j ^ info[0]) * width, width)
        keep[j * width : (j + 1) * width, :] = mm(low_t[info[4]], g_in[:, pl.ds(at, width)]).astype(BF)
    back, u1 = back_in[...], u1_in[...]
    small_out[1:2, :] = colsum(back * u1)
    small_out[2:3, :] = colsum(back)
    g_sum = norm_back(back * vec[3:4, :], u1, r1_in[:, 0:1])
    g_sum_out[...] = g_sum
    g_branch = g_sum.astype(BF)
    small_out[0:1, :] = colsum(g_branch.astype(F32))
    o = o_in[...]
    g_att = mm(g_branch, wo_in[...], NT).astype(BF)
    g_att_out[...] = g_att
    put_pieces(att_t, 0, o.T.astype(BF), info[2])
    wo_a[...] = mm(att_t[...], g_branch).astype(BF)
    head = lax.broadcasted_iota(jnp.int32, (16, width), 0)
    lane = lax.broadcasted_iota(jnp.int32, (16, width), 1)
    pick = jnp.where(lane // HD == head, 1.0, 0.0).astype(F32)
    dots_out[...] = lax.dot_general(
        pick, g_att.astype(F32) * o, NT, precision=lax.Precision.HIGHEST, preferred_element_type=F32
    )


def branch_back(order, info, o, u1, r1, back, g_in, low_t, wo, vec):
    tok, width = o.shape
    ff = g_in.shape[1]
    return ordered(
        branch_back_body,
        order,
        [SM] + [VM] * 8,
        (info, o, u1, r1, back, g_in, low_t, wo, vec,),
        "branch_back",
        out_specs=[VM] * 6,
        out_shape=[
            pltpu.HBM((ff // 2, width), BF),
            pltpu.HBM((tok, width), F32),
            pltpu.HBM((tok, width), BF),
            jax.ShapeDtypeStruct((16, tok), F32),
            jax.ShapeDtypeStruct((8, width), F32),
            pltpu.HBM((width, width), BF),
        ],
        scratch_shapes=[pltpu.VMEM((width, tok), BF)],
        cost_estimate=cost(2 * tok * width * (ff // 2 + 2 * width), 4 * width * ff),
        compiler_params=params(),
    )


def attend_back_body(q_in, k_in, v_in, g_in, bias, lse, dots, dq_out, dk_out, dv_out, kt, dqt):
    total = k_in.shape[1]
    step = 256
    per = step // BLK
    kt[...] = k_in[0].astype(F32).T.astype(BF)
    for pair in range(QUAD // 2):
        lanes = slice(pair * 128, pair * 128 + 128)
        qs = [half_mask(q_in[:, lanes], s) for s in range(2)]
        gs = [half_mask(g_in[:, lanes], s) for s in range(2)]
        dqs = [jnp.zeros((HD, q_in.shape[0]), F32) for _ in range(2)]
        for c in range(total // step):
            rows = slice(c * step, (c + 1) * step)
            kc = k_in[0, rows, lanes]
            vc = v_in[0, rows, lanes]
            dk = jnp.zeros((step, 128), F32)
            dv = jnp.zeros((step, 128), F32)
            for s in range(2):
                head = pair * 2 + s
                sc = mm(kc, qs[s], NT)
                dp = mm(vc, gs[s], NT)
                shift = bias[head, c * per : (c + 1) * per, :] - lse[0, head : head + 1, :]
                p = jnp.concatenate(
                    [jnp.exp(sc[b * BLK : (b + 1) * BLK, :] + shift[b : b + 1, :]) for b in range(per)], axis=0
                )
                ds = (p * (dp - dots[0, head : head + 1, :])).astype(BF)
                dv = dv + mm(p.astype(BF), gs[s])
                dk = dk + mm(ds, qs[s])
                dqs[s] = dqs[s] + mm(kt[head * HD : (head + 1) * HD, rows], ds)
            dk_out[0, rows, lanes] = dk.astype(BF)
            dv_out[0, rows, lanes] = dv.astype(BF)
        for s in range(2):
            head = pair * 2 + s
            dqt[head * HD : (head + 1) * HD, :] = dqs[s]
    dq_out[0] = (dqt[...].T * (1.0 / math.sqrt(HD))).astype(BF)


def attend_back(order, q, k, v, g, bias, lse, dots):
    tok, width = q.shape
    groups, total, cols = k.shape
    col = pl.BlockSpec((tok, cols), lambda i: (0, i))
    group = lambda r: pl.BlockSpec((1, r, cols), lambda i: (i, 0, 0))
    stat = pl.BlockSpec((1, QUAD, tok), lambda i: (i, 0, 0))
    return ordered(
        attend_back_body,
        order,
        [col, group(total), group(total), col]
        + [pl.BlockSpec((QUAD,) + bias.shape[1:], lambda i: (i, 0, 0)), stat, stat],
        (*(pltpu.with_memory_space_constraint(a, pltpu.HBM) for a in (q, k, v, g)), bias, lse, dots),
        "attend_back",
        grid=(groups,),
        out_specs=[group(tok), group(total), group(total)],
        out_shape=[jax.ShapeDtypeStruct((groups, r, cols), BF) for r in (tok, total, total)],
        scratch_shapes=[pltpu.VMEM((cols, total), BF), pltpu.VMEM((cols, tok), F32)],
        cost_estimate=cost(BACK_FLOPS, 1 << 20),
        compiler_params=params(),
    )


def weights_body(rows, smalls, info, wo_grad, *refs):
    n = len(rows)
    small_in, refs = refs[:smalls], refs[smalls:]
    groups = HEADS // QUAD
    dqs, dks, dvs = refs[:3]
    pieces = refs[3 : 3 + n]
    keep, send = refs[3 + n : 5 + n]
    x0, x1, tmp, small = refs[5 + n :]
    own = rows[0]
    start = 0
    for piece, count in zip(pieces, rows):
        t = piece[...].astype(F32).T.astype(BF)
        for p in range(t.shape[0] // 96):
            for xt, mix in ((x0, info[2]), (x1, info[3])):
                if start < own or xt is x1:
                    at = pl.multiple_of((p ^ mix) * 96, 16)
                    xt[pl.ds(at, 96), start : start + count] = t[p * 96 : (p + 1) * 96, :]
        start += count
    small[...] = jnp.zeros_like(small)
    cols = QUAD * HD
    width = keep.shape[1]
    for g in range(groups):
        lanes = slice(g * cols, (g + 1) * cols)
        small[0:1, lanes] = colsum(dqs[g].astype(F32))
        small[1:2, lanes] = colsum(dvs[g].astype(F32))
        tmp[0] = wo_grad[:, lanes]
        tmp[1] = mm(x0[...], dqs[g]).astype(BF)
        tmp[2] = mm(x1[...], dks[g]).astype(BF)
        tmp[3] = mm(x1[...], dvs[g]).astype(BF)
        for j in range(2):
            keep[j * width : (j + 1) * width, lanes] = tmp[j ^ info[0]]
            send[j * width : (j + 1) * width, lanes] = tmp[j ^ info[1]]
    tail = jnp.concatenate([r[...] for r in small_in] + [small[...]], axis=0).astype(BF)
    keep[2 * width :, :] = tail
    send[2 * width :, :] = tail


def weights(order, info, dqs, dks, dvs, wo_grad, pieces, smalls):
    rows = tuple(p.shape[0] for p in pieces)
    total = sum(rows)
    width = wo_grad.shape[0]
    _, tok, cols = dqs.shape
    half = pltpu.HBM((2 * width + 8 * (len(smalls) + 1), width), BF)
    count = 1 + len(smalls) + 3 + len(rows)
    return ordered(
        functools.partial(weights_body, rows, len(smalls)),
        order,
        [SM] + [VM] * count,
        (info, wo_grad, *smalls, dqs, dks, dvs, *pieces),
        "weights",
        out_specs=[VM] * 2,
        out_shape=[half, half],
        scratch_shapes=[
            pltpu.VMEM((width, tok), BF),
            pltpu.VMEM((width, total), BF),
            pltpu.VMEM((4, width, cols), BF),
            pltpu.VMEM((8, width), F32),
        ],
        cost_estimate=cost(2 * width * width * (tok + 2 * total), 4 * width * width * 4),
        compiler_params=params(),
    )


def token_body(starts, count, info, wq, wk, wv, g_sum, *refs):
    groups = HEADS // QUAD
    dqs, dks, dvs = refs[:3]
    own, outs = refs[3], refs[4:]
    cols = QUAD * HD

    def part(place):
        rows = pl.ds(place * count if isinstance(place, int) else pl.multiple_of(place * count, count), count)
        t = jnp.zeros((count, wq.shape[0]), F32)
        for g in range(groups):
            lanes = slice(g * cols, (g + 1) * cols)
            t = t + mm(dks[g, rows, :], wk[:, lanes], NT)
            t = t + mm(dvs[g, rows, :], wv[:, lanes], NT)
        return t

    t = part(0) + g_sum[...]
    for g in range(groups):
        t = t + mm(dqs[g], wq[:, g * cols : (g + 1) * cols], NT)
    own[...] = t
    for out, places in zip(outs, starts):
        for i, (base, sign) in enumerate(places):
            place = base if sign == 0 else base + sign * info[4]
            out[i * count : (i + 1) * count, :] = part(place).astype(BF)


def token_parts(order, starts, info, dqs, dks, dvs, wq, wk, wv, g_sum):
    tok, width = g_sum.shape
    return ordered(
        functools.partial(token_body, starts, tok),
        order,
        [SM] + [VM] * (4 + 3),
        (info, wq, wk, wv, g_sum, dqs, dks, dvs),
        "token_parts",
        out_specs=[VM] * (1 + len(starts)),
        out_shape=[jax.ShapeDtypeStruct((tok, width), F32)]
        + [jax.ShapeDtypeStruct((tok * len(p), width), BF) for p in starts],
        cost_estimate=cost(2 * width * width * 9 * tok, 4 * width * width * 4),
        compiler_params=params(),
    )


def unpack_body(kind, blocks, made, info, *refs):
    n = len(blocks)
    ins = refs[:n]
    refs = refs[n + made :]
    count = len(refs) - 2
    outs, wide, sems = refs[:count], refs[count], refs[count + 1]
    size = 96
    width = ins[0].shape[1]
    places = []
    for b, (ref, (side, j)) in enumerate(zip(ins, blocks)):
        for i in range(width // size):
            at = pl.multiple_of((i ^ info[5 + side]) * size, 32)
            wide[b, pl.ds(at, size), :] = ref[i * size : (i + 1) * size, :].astype(F32)
        chunk = info[side] ^ j
        if kind == "four":
            places.append([(chunk == c, outs[c]) for c in range(4)])
        else:
            at = pl.multiple_of(chunk * width, width)
            places.append([(None, outs[0].at[pl.ds(at, width), :] if kind == "rows" else outs[0].at[:, pl.ds(at, width)])])
        for when, out in places[b]:
            copy = pltpu.make_async_copy(wide.at[b], out, sems.at[b])
            if when is None:
                copy.start()
            else:
                pl.when(when)(copy.start)
    for b in range(n):
        for when, out in places[b]:
            copy = pltpu.make_async_copy(wide.at[b], out, sems.at[b])
            if when is None:
                copy.wait()
            else:
                pl.when(when)(copy.wait)


def unpack(order, kind, info, arrays, blocks, width, ff, made=()):
    shapes = {
        "rows": [(ff, width)],
        "cols": [(width, ff)],
        "four": [(width, width)] * 4,
    }[kind]
    return ordered(
        functools.partial(unpack_body, kind, blocks, len(made)),
        order,
        [SM] + [VM] * len(arrays) + [ANYWHERE] * len(made),
        (info, *arrays, *made),
        "unpack_" + kind,
        out_specs=[ANYWHERE] * len(shapes),
        out_shape=[jax.ShapeDtypeStruct(s, F32) for s in shapes],
        scratch_shapes=[pltpu.VMEM((len(arrays), width, width), F32), pltpu.SemaphoreType.DMA((len(arrays),))],
        input_output_aliases={1 + len(arrays) + i: i for i in range(len(made))},
        cost_estimate=cost(ff * width, 6 * ff * width),
        compiler_params=params(),
    )


def xor_permute(value, axis, mask):
    size = lax.axis_size(axis)
    return lax.ppermute(value, axis, [(i, i ^ mask) for i in range(size)])


def rows_at(count, index):
    return pl.BlockSpec((count, 768), lambda *_: (index, 0))


def in_hbm(array):
    return pltpu.with_memory_space_constraint(array, pltpu.HBM) if array.shape[0] > 1024 else array


def combine_body(ways, terms, extras, *refs):
    ins, outs = refs[: ways * terms + extras], refs[ways * terms + extras :]
    for w in range(ways):
        value = ins[w * terms][...].astype(F32)
        for r in ins[w * terms + 1 : (w + 1) * terms]:
            value = value + r[...].astype(F32)
        outs[w][: value.shape[0], :] = value.astype(BF)
    if extras:
        tail = (ins[ways * terms][...].astype(F32) + ins[ways * terms + 1][...].astype(F32)).astype(BF)
        for out in outs:
            out[out.shape[0] - tail.shape[0] :, :] = tail


def combine(order, count, ways, extras=()):
    width = ways[0][0][0].shape[1]
    terms = [t for way in ways for t in way]
    made = jax.ShapeDtypeStruct((count + (32 if extras else 0), width), BF)
    return ordered(
        functools.partial(combine_body, len(ways), len(ways[0]), len(extras)),
        order,
        [rows_at(count, i) for _, i in terms] + [rows_at(32, i) for _, i in extras],
        (*(in_hbm(a) for a, _ in terms), *(in_hbm(a) for a, _ in extras)),
        "combine",
        grid=(1,),
        out_specs=[pl.BlockSpec(made.shape, lambda *_: (0, 0))] * len(ways),
        out_shape=[made] * len(ways),
        cost_estimate=cost(EVENT_FLOPS, 1 << 20),
        compiler_params=params(),
    )


def finish_body(parts, extras, *refs):
    ins, outs = refs[: parts + extras], refs[parts + extras :]
    value = ins[0][...].astype(F32)
    for r in ins[1:parts]:
        value = value + r[...].astype(F32)
    outs[0][...] = value.astype(BF)
    if extras:
        outs[1][...] = ins[parts][...].astype(F32) + ins[parts + 1][...].astype(F32)


def finish(order, arrays, count, extras=()):
    width = arrays[0].shape[1]
    out = [jax.ShapeDtypeStruct((count, width), BF)]
    if extras:
        out.append(jax.ShapeDtypeStruct((32, width), F32))
    return ordered(
        functools.partial(finish_body, len(arrays), len(extras)),
        order,
        [rows_at(count, 0)] * len(arrays) + [rows_at(32, i) for _, i in extras],
        (*(in_hbm(a) for a in arrays), *(in_hbm(a) for a, _ in extras)),
        "finish",
        grid=(1,),
        out_specs=[pl.BlockSpec(o.shape, lambda *_: (0, 0)) for o in out],
        out_shape=out,
        cost_estimate=cost(EVENT_FLOPS, 1 << 20),
        compiler_params=params(),
    )


def token_sum_body(own, first, second, out):
    out[...] = own[...] + (first[...].astype(F32) + second[...].astype(F32))


def token_sum(order, own, first, second):
    tok, width = own.shape
    block = pl.BlockSpec((tok, width), lambda *_: (0, 0))
    return ordered(
        token_sum_body,
        order,
        [block] * 3,
        (own, first, second),
        "token_sum",
        grid=(1,),
        out_specs=block,
        out_shape=jax.ShapeDtypeStruct((tok, width), F32),
        cost_estimate=cost(EVENT_FLOPS, 1 << 20),
        compiler_params=params(),
    )


def stack_body(*refs):
    at = 0
    for r in refs[:-1]:
        refs[-1][at : at + r.shape[0], :] = r[...]
        at += r.shape[0]


def stack(order, arrays):
    rows, width = sum(a.shape[0] for a in arrays), arrays[0].shape[1]
    return ordered(
        stack_body,
        order,
        [VM] * len(arrays),
        (*arrays,),
        "stack",
        out_specs=VM,
        out_shape=jax.ShapeDtypeStruct((rows, width), arrays[0].dtype),
        cost_estimate=cost(EVENT_FLOPS, 1 << 20),
        compiler_params=params(),
    )


STAGES = (((1, 0), (2, 0)), ((2, 0), (1, 0)), ((0, 2), (0, 4)), ((0, 4), (0, 2)))


def swap(value, stage):
    shards = lax.axis_size("seq")
    pairs = []
    for b in range(lax.axis_size("batch")):
        of_shard, of_batch = STAGES[stage][b % 2]
        pairs += [(b * shards + s, (b ^ of_batch) * shards + (s ^ of_shard)) for s in range(shards)]
    return lax.ppermute(value, ("batch", "seq"), pairs)


class Order:
    def __init__(self):
        self.last = None


class Unit:
    def __init__(self, order, keep, got, rows):
        self.order, self.rows, self.stage = order, rows, 0
        self.parts = [keep, got]
        self.extra = [(a, rows // 32) for a in self.parts] if keep.shape[0] > rows else []

    def step(self):
        if self.stage < 4:
            half = self.rows // 2
            (sent,) = combine(self.order, half, [[(p, 1) for p in self.parts]], self.extra)
            got = swap(sent, self.stage)
            if self.extra:
                self.extra = [(sent, half // 32), (got, half // 32)]
            self.parts.append(got)
            self.rows = half
        else:
            if self.stage == 4:
                body, *tail = finish(self.order, self.parts, self.rows, self.extra)
                self.extra = tail[0] if tail else None
            else:
                body = stack(self.order, self.held)
            self.held = [body, swap(body, 7 - self.stage)]
        self.stage += 1

    def forward(self):
        self.others = [xor_permute(a, "batch", 1) for a in self.held]


def summed_plain(info, first, second, third, tokens, width, ff):
    axes = ("batch", "seq")

    def whole_sum(keep, send):
        part = lax.psum_scatter(jnp.concatenate([keep, send], axis=0), axes, scatter_dimension=0, tiled=True)
        return lax.all_gather(part, axes, axis=0, tiled=True)

    blocks = ((0, 0), (0, 1), (1, 0), (1, 1))

    def placed(kind, pair):
        total = whole_sum(*pair)
        return unpack(None, kind, info, [total[i * width : (i + 1) * width] for i in range(4)], blocks, width, ff)

    d_outer = placed("rows", first)
    d_inner = placed("cols", second)
    d_four = placed("four", third)
    return d_outer, d_inner, d_four, [xor_permute(t, "seq", k) for k, t in enumerate(tokens, 1)]


def gather_tokens(x, small):
    size = lax.axis_size("seq")
    if small:
        a = xor_permute(x, "seq", 1)
        b = xor_permute(x, "seq", 2)
        half = x.shape[0] // 2
        return [x, a, b, xor_permute(a[:half], "seq", 2), xor_permute(b[half:], "seq", 1)]
    return [x] + [xor_permute(x, "seq", k) for k in range(1, size)]


def multiplicity_bias(random_blocks, count, shard_index, shard_count, blocks_dev):
    order = shard_index ^ jnp.arange(shard_count, dtype=jnp.int32)
    key_ids = (order[:, None] * blocks_dev + jnp.arange(blocks_dev, dtype=jnp.int32)[None, :]).reshape(-1)
    query_ids = shard_index * blocks_dev + jnp.arange(blocks_dev, dtype=jnp.int32)
    near = (jnp.abs(key_ids[:, None] - query_ids[None, :]) <= 1).astype(jnp.int32)
    lead = (key_ids < count).astype(jnp.int32)
    picks = random_blocks.transpose(1, 0, 2)
    times = jnp.sum((picks[:, None, :, :] == key_ids[None, :, None, None]).astype(jnp.int32), axis=-1)
    times = times + near[None] + lead[None, :, None]
    times = jnp.where((query_ids < count)[None, None, :], 1, times)
    bias = jnp.where(times > 0, jnp.log(jnp.maximum(times, 1).astype(F32)), NEGATIVE)
    return jnp.repeat(bias, BLK, axis=2)


def on_device(
    tokens, cotangent, w_query, b_query, w_key, w_value, b_value, w_out, b_out, first_gain, first_shift,
    w_inner, b_inner, w_outer, b_outer, second_gain, second_shift, global_counts, random_blocks,
):
    _, tok, width = tokens.shape
    ff = w_inner.shape[1]
    blocks_dev = tok // BLK
    shard_count = lax.axis_size("seq")
    shard = lax.axis_index("seq")
    batch = lax.axis_index("batch")
    direct = shard_count == 4 and lax.axis_size("batch") == 8
    if direct:
        core, z = batch & 1, batch >> 1
        x_bit, y_bit = shard & 1, shard >> 1
        first = jnp.where(core == 0, x_bit, y_bit)
        low_z, high_z = z & 1, z >> 1
        mix_0, mix_1 = y_bit * 4 + low_z * 2 + high_z, x_bit * 4 + high_z * 2 + low_z
        info = [core * 2 + first, (1 - core) * 2 + (x_bit + y_bit - first), mix_0, mix_1, core]
        info += [jnp.where(core == 0, mix_0, mix_1), jnp.where(core == 0, mix_1, mix_0)]
        info = jnp.stack(info).astype(jnp.int32)
    else:
        info = jnp.array([0, 2, 0, 0, 0, 0, 0], jnp.int32)
    x = tokens.reshape(tok, width)
    vec = jnp.concatenate(
        [b_query, b_value, b_out, first_gain, first_shift, b_outer, second_gain, second_shift, b_inner]
    ).reshape(-1, width)
    bias = multiplicity_bias(random_blocks[0], global_counts[0], shard, shard_count, blocks_dev)
    pieces = gather_tokens(x, direct)
    rows = tuple(p.shape[0] for p in pieces)
    groups = HEADS // QUAD
    order = Order() if direct else None
    pairs = ((0, 0), (0, 1), (1, 0), (1, 1))
    q, k, v, o, lse = attend(order, pieces, w_query, w_key, w_value, vec, bias)
    layer_out, u1, r1, g_second, g_outer, slope, small_1, hid_t, send_1 = feed(
        order, info, o, x, cotangent.reshape(tok, width), w_out, w_inner, w_outer, vec
    )

    def exchange(value):
        return xor_permute(value, "batch", 1) if direct else value

    got_1 = exchange(send_1)
    keep_1, g_in, low_t, back, small_2, send_2 = inner_back(
        order, info, u1, g_second, g_outer, slope, hid_t, w_inner, w_outer, vec
    )
    if direct:
        one = Unit(order, keep_1, got_1, 2 * width)
        one.step()
    keep_2, g_sum, g_att, dots, small_3, wo_grad = branch_back(order, info, o, u1, r1, back, g_in, low_t, w_out, vec)
    dots = dots[:HEADS].reshape(groups, QUAD, tok)
    got_2 = exchange(send_2)

    def attend_step():
        return attend_back(order, q, k, v, g_att, bias, lse, dots)

    def weights_step():
        return weights(order, info, *backs, wo_grad, pieces, smalls)

    def token_step(starts):
        return token_parts(order, starts, info, *backs, w_query, w_key, w_value, g_sum)

    smalls = (small_1, small_2, small_3)
    if direct:
        two = Unit(order, keep_2, got_2, 2 * width)
        two.step()
        backs = attend_step()
        one.step()
        keep_3, send_3 = weights_step()
        three = Unit(order, keep_3, exchange(send_3), 2 * width)
        two.step()
        one.step()
        parts = token_step((((1, 1), (3, 0)), ((2, -1),)))
        got_a = swap(parts[1], 0)
        two.step()
        one.step()
        three.step()
        two.step()
        one.step()
        (relay,) = combine(order, tok, [[(parts[2], 0), (got_a, 1)]])
        got_b = swap(relay, 1)
        two.step()
        one.step()
        three.step()
        token_grad = token_sum(order, parts[0], got_a, got_b)
        two.step()
        one.step()
        three.step()
        two.step()
        one.step()
        three.step()
        two.step()
        three.step()
        three.step()
        one.forward()
        (d_outer,) = unpack(order, "rows", info, one.held + one.others, pairs, width, ff)
        three.step()
        two.forward()
        (d_inner,) = unpack(order, "cols", info, two.held + two.others, pairs, width, ff)
        three.step()
        three.others = [xor_permute(three.held[0], "batch", 1)]
        made = unpack(order, "four", info, [three.held[0], three.others[0]], pairs[::2], width, ff)
        three.held[1], *made = lax.optimization_barrier((three.held[1], *made))
        three.others.append(xor_permute(three.held[1], "batch", 1))
        made = unpack(order, "four", info, [three.held[1]], pairs[1:2], width, ff, made)
        d_out, d_query, d_key, d_value = unpack(order, "four", info, [three.others[1]], pairs[3:], width, ff, made)
        vectors = three.extra
    else:
        backs = attend_step()
        keep_3, send_3 = weights_step()
        parts = token_step(tuple(((i, 0),) for i in range(1, shard_count)))
        vectors = lax.psum(keep_3[2 * width :].astype(F32), ("batch", "seq"))
        third = (keep_3[: 2 * width], send_3[: 2 * width])
        d_outer, d_inner, d_four, got = summed_plain(
            info, (keep_1, send_1), (keep_2, send_2), third, parts[1:], width, ff
        )
        (d_outer,), (d_inner,) = d_outer, d_inner
        d_out, d_query, d_key, d_value = d_four
        token_grad = sum([g.astype(F32) for g in got], parts[0])
    return (
        layer_out.reshape(1, tok, width),
        token_grad.reshape(1, tok, width),
        d_query,
        vectors[24],
        d_key,
        d_value,
        vectors[25],
        d_out,
        vectors[16],
        vectors[17],
        vectors[18],
        d_inner,
        vectors[8:12].reshape(-1),
        d_outer,
        vectors[3],
        vectors[4],
        vectors[5],
    )


def solution(mesh):
    token_spec = P("batch", "seq", None)
    placed = (token_spec, token_spec) + (P(),) * 15 + (P("batch"), P("batch", "seq", None, None))
    return jax.shard_map(
        on_device,
        mesh=mesh,
        in_specs=placed,
        out_specs=(token_spec, token_spec) + (P(),) * 15,
        check_vma=False,
    )
```

```python
import functools
import math

import jax
import jax.numpy as jnp
from jax import lax
from jax.experimental import pallas as pl
from jax.experimental.pallas import tpu as pltpu
from jax.sharding import PartitionSpec as P

HEADS = 12
HD = 64
BLK = 64
GMAX = 4
QUAD = 4
EPSILON = 1e-06
NEGATIVE = -1e30
BF = jnp.bfloat16
F32 = jnp.float32
VMEM_BYTES = 24 * 1024 * 1024
EVENT_FLOPS = 43 * 10**6
BACK_FLOPS = 5 * 10**7

NN = (((1,), (0,)), ((), ()))
NT = (((1,), (1,)), ((), ()))
TN = (((0,), (0,)), ((), ()))


def mm(a, b, dims=NN):
    return lax.dot_general(a, b, dims, preferred_element_type=F32)


def params(**kw):
    return pltpu.CompilerParams(vmem_limit_bytes=VMEM_BYTES, **kw)


def cost(flops, bytes_accessed, exps=0):
    return pl.CostEstimate(flops=flops * 100, bytes_accessed=bytes_accessed * 100, transcendentals=exps * 100)


def ordered(body, order, in_specs, args, name, out_specs, out_shape, **kw):
    if order is None:
        return pl.pallas_call(
            body, in_specs=in_specs, out_specs=out_specs, out_shape=out_shape, name=name, **kw
        )(*args)
    one = not isinstance(out_shape, (list, tuple))
    specs, shapes = ([out_specs], [out_shape]) if one else (list(out_specs), list(out_shape))
    marks = [] if order.last is None else [order.last]
    n, made = len(args), len(shapes)
    mark = jax.ShapeDtypeStruct((8, 128), F32)

    def kernel(*refs):
        outs = refs[n + len(marks) :]
        outs[made][...] = jnp.zeros_like(outs[made])
        body(*refs[:n], *outs[:made], *outs[made + 1 :])

    mark_spec = pl.BlockSpec((8, 128), lambda *_: (0, 0))
    *out, order.last = pl.pallas_call(
        kernel,
        in_specs=list(in_specs) + [pl.BlockSpec(memory_space=pl.ANY)] * len(marks),
        out_specs=specs + [mark_spec],
        out_shape=shapes + [mark],
        name=name,
        **kw,
    )(*args, *marks)
    return out[0] if one else out


def whole(shape):
    return pl.BlockSpec(shape, lambda *_: (0,) * len(shape))


def half_mask(values, side):
    lane = lax.broadcasted_iota(jnp.int32, values.shape, 1)
    keep = lane < HD if side == 0 else lane >= HD
    return jnp.where(keep, values, jnp.zeros_like(values))


def attend_body(rows, *refs):
    n = len(rows)
    pieces = refs[:n]
    wq, wk, wv, vec, bias = refs[n : n + 5]
    q_out, k_out, v_out, o_out, lse_out = refs[n + 5 : n + 10]
    vt, sc, ot = refs[n + 10 :]
    q = (mm(pieces[0][...], wq[...]) + vec[0:1, :]).astype(BF)
    q_out[...] = (q.astype(F32) * (1.0 / math.sqrt(HD))).astype(BF)
    start = 0
    for piece, count in zip(pieces, rows):
        x = piece[...]
        k_out[0, start : start + count, :] = mm(x, wk[...]).astype(BF)
        v = mm(x, wv[...]) + vec[1:2, :]
        v_out[0, start : start + count, :] = v.astype(BF)
        vt[:, start : start + count] = v.astype(BF).T
        start += count
    total = start
    step = 256
    per = step // BLK
    for head in range(QUAD):
        lanes = slice(head // 2 * 128, head // 2 * 128 + 128)
        qh = half_mask(q_out[:, lanes], head % 2)
        top = jnp.full((1, qh.shape[0]), NEGATIVE, F32)
        for c in range(total // step):
            part = mm(k_out[0, c * step : (c + 1) * step, lanes], qh, NT)
            for b in range(per):
                row = bias[head, c * per + b : c * per + b + 1, :]
                s = part[b * BLK : (b + 1) * BLK, :] + row
                sc[c * step + b * BLK : c * step + (b + 1) * BLK, :] = s
                top = jnp.maximum(top, jnp.max(s, axis=0, keepdims=True))
        acc = jnp.zeros((HD, qh.shape[0]), F32)
        norm = jnp.zeros((1, qh.shape[0]), F32)
        for c in range(total // step):
            e = jnp.exp(sc[c * step : (c + 1) * step, :] - top)
            norm = norm + jnp.sum(e, axis=0, keepdims=True)
            acc = acc + mm(vt[head * HD : (head + 1) * HD, c * step : (c + 1) * step], e.astype(BF))
        ot[head * HD : (head + 1) * HD, :] = acc / norm
        lse_out[0, head : head + 1, :] = top + jnp.log(norm)
    o_out[...] = ot[...].T


def attend(order, pieces, wq, wk, wv, vec, bias):
    rows = tuple(p.shape[0] for p in pieces)
    total = sum(rows)
    tok, width = pieces[0].shape
    groups = HEADS // QUAD
    cols = QUAD * HD
    col = lambda r: pl.BlockSpec((r, cols), lambda g: (0, g))
    return ordered(
        functools.partial(attend_body, rows),
        order,
        [whole((r, width)) for r in rows]
        + [col(width), col(width), col(width), col(vec.shape[0])]
        + [pl.BlockSpec((QUAD,) + bias.shape[1:], lambda g: (g, 0, 0))],
        (*pieces, *(pltpu.with_memory_space_constraint(w, pltpu.HBM) for w in (wq, wk, wv)), vec, bias),
        "attend",
        grid=(groups,),
        out_specs=[
            col(tok),
            pl.BlockSpec((1, total, cols), lambda g: (g, 0, 0)),
            pl.BlockSpec((1, total, cols), lambda g: (g, 0, 0)),
            col(tok),
            pl.BlockSpec((1, QUAD, tok), lambda g: (g, 0, 0)),
        ],
        out_shape=[
            pltpu.HBM((tok, width), BF),
            pltpu.HBM((groups, total, cols), BF),
            pltpu.HBM((groups, total, cols), BF),
            jax.ShapeDtypeStruct((tok, width), F32),
            jax.ShapeDtypeStruct((groups, QUAD, tok), F32),
        ],
        scratch_shapes=[
            pltpu.VMEM((cols, total), BF),
            pltpu.VMEM((total, tok), F32),
            pltpu.VMEM((cols, tok), F32),
        ],
        cost_estimate=cost(2 * total * 256 * (2 * HEADS * tok + 3 * width * 2), 4 * total * width * 2, HEADS * tok * total),
        compiler_params=params(),
    )


def norm_stats(values):
    mean = jnp.mean(values, axis=-1, keepdims=True)
    centred = values - mean
    r = lax.rsqrt(jnp.mean(centred * centred, axis=-1, keepdims=True) + EPSILON)
    return centred * r, r


def norm_back(e, u, r):
    return r * (e - jnp.mean(e, axis=-1, keepdims=True) - u * jnp.mean(e * u, axis=-1, keepdims=True))


def colsum(values):
    return jnp.sum(values, axis=0, keepdims=True)


def put_pieces(dst, base, block, mix, size=96):
    for p in range(block.shape[0] // size):
        at = pl.multiple_of(base + (p ^ mix) * size, 16)
        dst[pl.ds(at, size), :] = block[p * size : (p + 1) * size, :]


def feed_body(
    info, o_in, x_in, cot_in, wo, wi, wu, vec,
    layer_out, u1_out, r1_out, g_second_out, g_outer_out, slope, small_out, hid_t, send,
):
    small_out[...] = jnp.zeros_like(small_out)
    width = wo.shape[0]
    chunks = wi.shape[1] // width
    b_out, fg, fs, b_outer, sg, ss = (vec[i : i + 1, :] for i in range(2, 8))
    att = o_in[...].astype(BF)
    first_in = x_in[...].astype(F32) + (mm(att, wo[...]) + b_out)
    u1, r1 = norm_stats(first_in)
    u1_out[...] = u1
    r1_out[...] = jnp.broadcast_to(r1, r1_out.shape)
    first = u1 * fg + fs
    low = first.astype(BF)
    out = jnp.zeros_like(first)
    for j in range(chunks):
        cols = slice(j * width, (j + 1) * width)
        v = mm(low, wi[:, cols]) + vec[8 + j : 9 + j, :]
        t = jnp.tanh(0.7978845608028654 * (v + 0.044715 * v * v * v))
        h = 0.5 * v * (1.0 + t)
        slope[:, cols] = 0.5 * (1.0 + t) + 0.5 * v * (1.0 - t * t) * (
            0.7978845608028654 * (1.0 + 3.0 * 0.044715 * v * v)
        )
        out = out + mm(h.astype(BF), wu[cols, :])
        put_pieces(hid_t, j * width, h.astype(BF).T, info[2 + 2 * j // chunks])
    u2, r2 = norm_stats(first + (out + b_outer))
    layer_out[...] = (u2 * sg + ss).astype(BF)
    cot = cot_in[...].astype(F32)
    small_out[4:5, :] = colsum(cot * u2)
    small_out[5:6, :] = colsum(cot)
    g_second = norm_back(cot * sg, u2, r2)
    g_second_out[...] = g_second
    g_outer = g_second.astype(BF)
    g_outer_out[...] = g_outer
    small_out[3:4, :] = colsum(g_outer.astype(F32))
    for j in range(chunks // 2):
        at = pl.multiple_of((j ^ info[1]) * width, width)
        send[j * width : (j + 1) * width, :] = mm(hid_t[pl.ds(at, width), :], g_outer).astype(BF)


VM = pl.BlockSpec(memory_space=pltpu.VMEM)
SM = pl.BlockSpec(memory_space=pltpu.SMEM)
ANYWHERE = pl.BlockSpec(memory_space=pl.ANY)


def feed(order, info, o, x, cot, wo, wi, wu, vec):
    tok, width = x.shape
    ff = wi.shape[1]
    return ordered(
        feed_body,
        order,
        [SM] + [VM] * 7,
        (info, o, x, cot, wo, wi, wu, vec,),
        "feed",
        out_specs=[VM] * 9,
        out_shape=[
            jax.ShapeDtypeStruct((tok, width), BF),
            jax.ShapeDtypeStruct((tok, width), F32),
            jax.ShapeDtypeStruct((tok, 128), F32),
            jax.ShapeDtypeStruct((tok, width), F32),
            jax.ShapeDtypeStruct((tok, width), BF),
            jax.ShapeDtypeStruct((tok, ff), F32),
            jax.ShapeDtypeStruct((8, width), F32),
            jax.ShapeDtypeStruct((ff, tok), BF),
            pltpu.HBM((ff // 2, width), BF),
        ],
        cost_estimate=cost(2 * tok * width * (5 * ff // 2 + width), 4 * (width * ff * 2), tok * ff),
        compiler_params=params(),
    )


def inner_back_body(
    info, u1_in, g_second_in, g_outer_in, slope, hid_t, wi, wu, vec,
    keep, g_in, low_t, back_out, small_out, send,
):
    small_out[...] = jnp.zeros_like(small_out)
    width = wi.shape[0]
    chunks = wi.shape[1] // width
    g_outer = g_outer_in[...]
    for j in range(chunks // 2):
        at = pl.multiple_of((j ^ info[0]) * width, width)
        keep[j * width : (j + 1) * width, :] = mm(hid_t[pl.ds(at, width), :], g_outer).astype(BF)
    flat_t = (u1_in[...] * vec[3:4, :] + vec[4:5, :]).astype(BF).T
    for c in range(2):
        put_pieces(low_t.at[c], 0, flat_t, info[2 + c])
    back = g_second_in[...]
    for j in range(chunks):
        cols = slice(j * width, (j + 1) * width)
        gi = (mm(g_outer, wu[cols, :], NT) * slope[:, cols]).astype(BF)
        g_in[:, cols] = gi
        small_out[j : j + 1, :] = colsum(gi.astype(F32))
        back = back + mm(gi, wi[:, cols], NT)
    back_out[...] = back
    for j in range(chunks // 2):
        at = pl.multiple_of((j ^ info[1]) * width, width)
        send[j * width : (j + 1) * width, :] = mm(low_t[1 - info[4]], g_in[:, pl.ds(at, width)]).astype(BF)


def inner_back(order, info, u1, g_second, g_outer, slope, hid_t, wi, wu, vec):
    tok, width = u1.shape
    ff = wi.shape[1]
    half = pltpu.HBM((ff // 2, width), BF)
    return ordered(
        inner_back_body,
        order,
        [SM] + [VM] * 8,
        (info, u1, g_second, g_outer, slope, hid_t, wi, wu, vec,),
        "inner_back",
        out_specs=[VM] * 6,
        out_shape=[
            half,
            jax.ShapeDtypeStruct((tok, ff), BF),
            jax.ShapeDtypeStruct((2, width, tok), BF),
            jax.ShapeDtypeStruct((tok, width), F32),
            jax.ShapeDtypeStruct((8, width), F32),
            half,
        ],
        cost_estimate=cost(2 * tok * width * 3 * ff, 4 * (width * ff * 2)),
        compiler_params=params(),
    )


def branch_back_body(
    info, o_in, u1_in, r1_in, back_in, g_in, low_t, wo_in, vec,
    keep, g_sum_out, g_att_out, dots_out, small_out, wo_a,
    att_t,
):
    small_out[...] = jnp.zeros_like(small_out)
    width = wo_in.shape[0]
    for j in range(keep.shape[0] // width):
        at = pl.multiple_of((j ^ info[0]) * width, width)
        keep[j * width : (j + 1) * width, :] = mm(low_t[info[4]], g_in[:, pl.ds(at, width)]).astype(BF)
    back, u1 = back_in[...], u1_in[...]
    small_out[1:2, :] = colsum(back * u1)
    small_out[2:3, :] = colsum(back)
    g_sum = norm_back(back * vec[3:4, :], u1, r1_in[:, 0:1])
    g_sum_out[...] = g_sum
    g_branch = g_sum.astype(BF)
    small_out[0:1, :] = colsum(g_branch.astype(F32))
    o = o_in[...]
    g_att = mm(g_branch, wo_in[...], NT).astype(BF)
    g_att_out[...] = g_att
    put_pieces(att_t, 0, o.astype(BF).T, info[2])
    wo_a[...] = mm(att_t[...], g_branch).astype(BF)
    head = lax.broadcasted_iota(jnp.int32, (16, width), 0)
    lane = lax.broadcasted_iota(jnp.int32, (16, width), 1)
    pick = jnp.where(lane // HD == head, 1.0, 0.0).astype(F32)
    dots_out[...] = lax.dot_general(
        pick, g_att.astype(F32) * o, NT, precision=lax.Precision.HIGHEST, preferred_element_type=F32
    )


def branch_back(order, info, o, u1, r1, back, g_in, low_t, wo, vec):
    tok, width = o.shape
    ff = g_in.shape[1]
    return ordered(
        branch_back_body,
        order,
        [SM] + [VM] * 8,
        (info, o, u1, r1, back, g_in, low_t, wo, vec,),
        "branch_back",
        out_specs=[VM] * 6,
        out_shape=[
            pltpu.HBM((ff // 2, width), BF),
            pltpu.HBM((tok, width), F32),
            pltpu.HBM((tok, width), BF),
            jax.ShapeDtypeStruct((16, tok), F32),
            jax.ShapeDtypeStruct((8, width), F32),
            pltpu.HBM((width, width), BF),
        ],
        scratch_shapes=[pltpu.VMEM((width, tok), BF)],
        cost_estimate=cost(2 * tok * width * (ff // 2 + 2 * width), 4 * width * ff),
        compiler_params=params(),
    )


def attend_back_body(q_in, k_in, v_in, g_in, bias, lse, dots, dq_out, dk_out, dv_out, kt, dqt):
    total = k_in.shape[1]
    step = 256
    per = step // BLK
    kt[...] = k_in[0].T
    for pair in range(QUAD // 2):
        lanes = slice(pair * 128, pair * 128 + 128)
        qs = [half_mask(q_in[:, lanes], s) for s in range(2)]
        gs = [half_mask(g_in[:, lanes], s) for s in range(2)]
        dqs = [jnp.zeros((HD, q_in.shape[0]), F32) for _ in range(2)]
        for c in range(total // step):
            rows = slice(c * step, (c + 1) * step)
            kc = k_in[0, rows, lanes]
            vc = v_in[0, rows, lanes]
            dk = jnp.zeros((step, 128), F32)
            dv = jnp.zeros((step, 128), F32)
            for s in range(2):
                head = pair * 2 + s
                sc = mm(kc, qs[s], NT)
                dp = mm(vc, gs[s], NT)
                shift = bias[head, c * per : (c + 1) * per, :] - lse[0, head : head + 1, :]
                p = jnp.concatenate(
                    [jnp.exp(sc[b * BLK : (b + 1) * BLK, :] + shift[b : b + 1, :]) for b in range(per)], axis=0
                )
                ds = (p * (dp - dots[0, head : head + 1, :])).astype(BF)
                dv = dv + mm(p.astype(BF), gs[s])
                dk = dk + mm(ds, qs[s])
                dqs[s] = dqs[s] + mm(kt[head * HD : (head + 1) * HD, rows], ds)
            dk_out[0, rows, lanes] = dk.astype(BF)
            dv_out[0, rows, lanes] = dv.astype(BF)
        for s in range(2):
            head = pair * 2 + s
            dqt[head * HD : (head + 1) * HD, :] = dqs[s]
    dq_out[0] = (dqt[...].T * (1.0 / math.sqrt(HD))).astype(BF)


def attend_back(order, q, k, v, g, bias, lse, dots):
    tok, width = q.shape
    groups, total, cols = k.shape
    col = pl.BlockSpec((tok, cols), lambda i: (0, i))
    group = lambda r: pl.BlockSpec((1, r, cols), lambda i: (i, 0, 0))
    stat = pl.BlockSpec((1, QUAD, tok), lambda i: (i, 0, 0))
    return ordered(
        attend_back_body,
        order,
        [col, group(total), group(total), col]
        + [pl.BlockSpec((QUAD,) + bias.shape[1:], lambda i: (i, 0, 0)), stat, stat],
        (*(pltpu.with_memory_space_constraint(a, pltpu.HBM) for a in (q, k, v, g)), bias, lse, dots),
        "attend_back",
        grid=(groups,),
        out_specs=[group(tok), group(total), group(total)],
        out_shape=[jax.ShapeDtypeStruct((groups, r, cols), BF) for r in (tok, total, total)],
        scratch_shapes=[pltpu.VMEM((cols, total), BF), pltpu.VMEM((cols, tok), F32)],
        cost_estimate=cost(BACK_FLOPS, 1 << 20),
        compiler_params=params(),
    )


def weights_body(rows, smalls, info, wo_grad, *refs):
    n = len(rows)
    small_in, refs = refs[:smalls], refs[smalls:]
    groups = HEADS // QUAD
    dqs, dks, dvs = refs[:3]
    pieces = refs[3 : 3 + n]
    keep, send = refs[3 + n : 5 + n]
    x0, x1, tmp, small = refs[5 + n :]
    own = rows[0]
    start = 0
    for piece, count in zip(pieces, rows):
        t = piece[...].T
        for p in range(t.shape[0] // 96):
            for xt, mix in ((x0, info[2]), (x1, info[3])):
                if start < own or xt is x1:
                    at = pl.multiple_of((p ^ mix) * 96, 16)
                    xt[pl.ds(at, 96), start : start + count] = t[p * 96 : (p + 1) * 96, :]
        start += count
    small[...] = jnp.zeros_like(small)
    cols = QUAD * HD
    width = keep.shape[1]
    for g in range(groups):
        lanes = slice(g * cols, (g + 1) * cols)
        small[0:1, lanes] = colsum(dqs[g].astype(F32))
        small[1:2, lanes] = colsum(dvs[g].astype(F32))
        tmp[0] = wo_grad[:, lanes]
        tmp[1] = mm(x0[...], dqs[g]).astype(BF)
        tmp[2] = mm(x1[...], dks[g]).astype(BF)
        tmp[3] = mm(x1[...], dvs[g]).astype(BF)
        for j in range(2):
            keep[j * width : (j + 1) * width, lanes] = tmp[j ^ info[0]]
            send[j * width : (j + 1) * width, lanes] = tmp[j ^ info[1]]
    tail = jnp.concatenate([r[...] for r in small_in] + [small[...]], axis=0).astype(BF)
    keep[2 * width :, :] = tail
    send[2 * width :, :] = tail


def weights(order, info, dqs, dks, dvs, wo_grad, pieces, smalls):
    rows = tuple(p.shape[0] for p in pieces)
    total = sum(rows)
    width = wo_grad.shape[0]
    _, tok, cols = dqs.shape
    half = pltpu.HBM((2 * width + 8 * (len(smalls) + 1), width), BF)
    count = 1 + len(smalls) + 3 + len(rows)
    return ordered(
        functools.partial(weights_body, rows, len(smalls)),
        order,
        [SM] + [VM] * count,
        (info, wo_grad, *smalls, dqs, dks, dvs, *pieces),
        "weights",
        out_specs=[VM] * 2,
        out_shape=[half, half],
        scratch_shapes=[
            pltpu.VMEM((width, tok), BF),
            pltpu.VMEM((width, total), BF),
            pltpu.VMEM((4, width, cols), BF),
            pltpu.VMEM((8, width), F32),
        ],
        cost_estimate=cost(2 * width * width * (tok + 2 * total), 4 * width * width * 4),
        compiler_params=params(),
    )


def token_body(starts, count, info, wq, wk, wv, g_sum, *refs):
    groups = HEADS // QUAD
    dqs, dks, dvs = refs[:3]
    own, outs = refs[3], refs[4:]
    cols = QUAD * HD

    def part(place):
        rows = pl.ds(place * count if isinstance(place, int) else pl.multiple_of(place * count, count), count)
        t = jnp.zeros((count, wq.shape[0]), F32)
        for g in range(groups):
            lanes = slice(g * cols, (g + 1) * cols)
            t = t + mm(dks[g, rows, :], wk[:, lanes], NT)
            t = t + mm(dvs[g, rows, :], wv[:, lanes], NT)
        return t

    t = part(0) + g_sum[...]
    for g in range(groups):
        t = t + mm(dqs[g], wq[:, g * cols : (g + 1) * cols], NT)
    own[...] = t
    for out, places in zip(outs, starts):
        for i, (base, sign) in enumerate(places):
            place = base if sign == 0 else base + sign * info[4]
            out[i * count : (i + 1) * count, :] = part(place).astype(BF)


def token_parts(order, starts, info, dqs, dks, dvs, wq, wk, wv, g_sum):
    tok, width = g_sum.shape
    return ordered(
        functools.partial(token_body, starts, tok),
        order,
        [SM] + [VM] * (4 + 3),
        (info, wq, wk, wv, g_sum, dqs, dks, dvs),
        "token_parts",
        out_specs=[VM] * (1 + len(starts)),
        out_shape=[jax.ShapeDtypeStruct((tok, width), F32)]
        + [jax.ShapeDtypeStruct((tok * len(p), width), BF) for p in starts],
        cost_estimate=cost(2 * width * width * 9 * tok, 4 * width * width * 4),
        compiler_params=params(),
    )


def unpack_body(kind, blocks, made, info, *refs):
    n = len(blocks)
    ins = refs[:n]
    refs = refs[n + made :]
    count = len(refs) - 2
    outs, wide, sems = refs[:count], refs[count], refs[count + 1]
    size = 96
    rows, width = ins[0].shape
    pieces = rows // size
    copies = []
    for b, (ref, (side, j, half)) in enumerate(zip(ins, blocks)):
        mix = info[5 + side]
        for i in range(pieces):
            at = pl.multiple_of((i ^ (mix & (pieces - 1))) * size, 32)
            wide[b, pl.ds(at, size), :] = ref[i * size : (i + 1) * size, :].astype(F32)
        chunk = info[side] ^ j
        if kind == "four":
            at = pl.multiple_of((half ^ (mix // pieces)) * rows, rows)
            targets = [(chunk == c, outs[c].at[pl.ds(at, rows), :]) for c in range(4)]
        else:
            at = pl.multiple_of(chunk * width, width)
            targets = [(None, outs[0].at[pl.ds(at, width), :] if kind == "rows" else outs[0].at[:, pl.ds(at, width)])]
        for when, out in targets:
            copy = pltpu.make_async_copy(wide.at[b], out, sems.at[b])
            copies.append((when, copy))
            if when is None:
                copy.start()
            else:
                pl.when(when)(copy.start)
    for when, copy in copies:
        if when is None:
            copy.wait()
        else:
            pl.when(when)(copy.wait)


def unpack(order, kind, info, arrays, blocks, width, ff, made=()):
    shapes = {
        "rows": [(ff, width)],
        "cols": [(width, ff)],
        "four": [(width, width)] * 4,
    }[kind]
    return ordered(
        functools.partial(unpack_body, kind, blocks, len(made)),
        order,
        [SM] + [VM] * len(arrays) + [ANYWHERE] * len(made),
        (info, *arrays, *made),
        "unpack_" + kind,
        out_specs=[ANYWHERE] * len(shapes),
        out_shape=[jax.ShapeDtypeStruct(s, F32) for s in shapes],
        scratch_shapes=[
            pltpu.VMEM((len(arrays),) + arrays[0].shape, F32),
            pltpu.SemaphoreType.DMA((len(arrays),)),
        ],
        input_output_aliases={1 + len(arrays) + i: i for i in range(len(made))},
        cost_estimate=cost(ff * width, 6 * ff * width),
        compiler_params=params(),
    )


def xor_permute(value, axis, mask):
    size = lax.axis_size(axis)
    return lax.ppermute(value, axis, [(i, i ^ mask) for i in range(size)])


def rows_at(count, index):
    return pl.BlockSpec((count, 768), lambda *_: (index, 0))


def in_hbm(array):
    return pltpu.with_memory_space_constraint(array, pltpu.HBM) if array.shape[0] > 1024 else array


def combine_body(ways, terms, extras, *refs):
    ins, outs = refs[: ways * terms + extras], refs[ways * terms + extras :]
    for w in range(ways):
        value = ins[w * terms][...].astype(F32)
        for r in ins[w * terms + 1 : (w + 1) * terms]:
            value = value + r[...].astype(F32)
        outs[w][: value.shape[0], :] = value.astype(BF)
    if extras:
        tail = (ins[ways * terms][...].astype(F32) + ins[ways * terms + 1][...].astype(F32)).astype(BF)
        for out in outs:
            out[out.shape[0] - tail.shape[0] :, :] = tail


def combine(order, count, ways, extras=()):
    width = ways[0][0][0].shape[1]
    terms = [t for way in ways for t in way]
    made = jax.ShapeDtypeStruct((count + (32 if extras else 0), width), BF)
    return ordered(
        functools.partial(combine_body, len(ways), len(ways[0]), len(extras)),
        order,
        [rows_at(count, i) for _, i in terms] + [rows_at(32, i) for _, i in extras],
        (*(in_hbm(a) for a, _ in terms), *(in_hbm(a) for a, _ in extras)),
        "combine",
        grid=(1,),
        out_specs=[pl.BlockSpec(made.shape, lambda *_: (0, 0))] * len(ways),
        out_shape=[made] * len(ways),
        cost_estimate=cost(EVENT_FLOPS, 1 << 20),
        compiler_params=params(),
    )


def finish_body(parts, extras, *refs):
    ins, outs = refs[: parts + extras], refs[parts + extras :]
    value = ins[0][...].astype(F32)
    for r in ins[1:parts]:
        value = value + r[...].astype(F32)
    outs[0][...] = value.astype(BF)
    if extras:
        outs[1][...] = ins[parts][...].astype(F32) + ins[parts + 1][...].astype(F32)


def finish(order, arrays, count, extras=()):
    width = arrays[0].shape[1]
    out = [jax.ShapeDtypeStruct((count, width), BF)]
    if extras:
        out.append(jax.ShapeDtypeStruct((32, width), F32))
    return ordered(
        functools.partial(finish_body, len(arrays), len(extras)),
        order,
        [rows_at(count, 0)] * len(arrays) + [rows_at(32, i) for _, i in extras],
        (*(in_hbm(a) for a in arrays), *(in_hbm(a) for a, _ in extras)),
        "finish",
        grid=(1,),
        out_specs=[pl.BlockSpec(o.shape, lambda *_: (0, 0)) for o in out],
        out_shape=out,
        cost_estimate=cost(EVENT_FLOPS, 1 << 20),
        compiler_params=params(),
    )


def token_sum_body(own, first, second, out):
    out[...] = own[...] + (first[...].astype(F32) + second[...].astype(F32))


def token_sum(order, own, first, second):
    tok, width = own.shape
    block = pl.BlockSpec((tok, width), lambda *_: (0, 0))
    return ordered(
        token_sum_body,
        order,
        [block] * 3,
        (own, first, second),
        "token_sum",
        grid=(1,),
        out_specs=block,
        out_shape=jax.ShapeDtypeStruct((tok, width), F32),
        cost_estimate=cost(EVENT_FLOPS, 1 << 20),
        compiler_params=params(),
    )


def stack_body(*refs):
    at = 0
    for r in refs[:-1]:
        refs[-1][at : at + r.shape[0], :] = r[...]
        at += r.shape[0]


def stack(order, arrays):
    rows, width = sum(a.shape[0] for a in arrays), arrays[0].shape[1]
    return ordered(
        stack_body,
        order,
        [VM] * len(arrays),
        (*arrays,),
        "stack",
        out_specs=VM,
        out_shape=jax.ShapeDtypeStruct((rows, width), arrays[0].dtype),
        cost_estimate=cost(EVENT_FLOPS, 1 << 20),
        compiler_params=params(),
    )


STAGES = (((1, 0), (2, 0)), ((2, 0), (1, 0)), ((0, 2), (0, 4)), ((0, 4), (0, 2)))


def swap(value, stage):
    shards = lax.axis_size("seq")
    pairs = []
    for b in range(lax.axis_size("batch")):
        of_shard, of_batch = STAGES[stage][b % 2]
        pairs += [(b * shards + s, (b ^ of_batch) * shards + (s ^ of_shard)) for s in range(shards)]
    return lax.ppermute(value, ("batch", "seq"), pairs)


class Order:
    def __init__(self):
        self.last = None


class Unit:
    def __init__(self, order, keep, got, rows):
        self.order, self.rows, self.stage = order, rows, 0
        self.parts = [keep, got]
        self.extra = [(a, rows // 32) for a in self.parts] if keep.shape[0] > rows else []

    def step(self):
        if self.stage < 4:
            half = self.rows // 2
            (sent,) = combine(self.order, half, [[(p, 1) for p in self.parts]], self.extra)
            got = swap(sent, self.stage)
            if self.extra:
                self.extra = [(sent, half // 32), (got, half // 32)]
            self.parts.append(got)
            self.rows = half
        else:
            if self.stage == 4:
                body, *tail = finish(self.order, self.parts, self.rows, self.extra)
                self.extra = tail[0] if tail else None
            else:
                body = stack(self.order, self.held)
            self.held = [body, swap(body, 7 - self.stage)]
        self.stage += 1

    def forward(self):
        self.others = [xor_permute(a, "batch", 1) for a in self.held]


def summed_plain(info, first, second, third, tokens, width, ff):
    axes = ("batch", "seq")

    def whole_sum(keep, send):
        part = lax.psum_scatter(jnp.concatenate([keep, send], axis=0), axes, scatter_dimension=0, tiled=True)
        return lax.all_gather(part, axes, axis=0, tiled=True)

    blocks = ((0, 0, 0), (0, 1, 0), (1, 0, 0), (1, 1, 0))

    def placed(kind, pair):
        total = whole_sum(*pair)
        return unpack(None, kind, info, [total[i * width : (i + 1) * width] for i in range(4)], blocks, width, ff)

    d_outer = placed("rows", first)
    d_inner = placed("cols", second)
    d_four = placed("four", third)
    return d_outer, d_inner, d_four, [xor_permute(t, "seq", k) for k, t in enumerate(tokens, 1)]


def gather_tokens(x, small):
    size = lax.axis_size("seq")
    if small:
        a = xor_permute(x, "seq", 1)
        b = xor_permute(x, "seq", 2)
        half = x.shape[0] // 2
        return [x, a, b, xor_permute(a[:half], "seq", 2), xor_permute(b[half:], "seq", 1)]
    return [x] + [xor_permute(x, "seq", k) for k in range(1, size)]


def multiplicity_bias(random_blocks, count, shard_index, shard_count, blocks_dev):
    order = shard_index ^ jnp.arange(shard_count, dtype=jnp.int32)
    key_ids = (order[:, None] * blocks_dev + jnp.arange(blocks_dev, dtype=jnp.int32)[None, :]).reshape(-1)
    query_ids = shard_index * blocks_dev + jnp.arange(blocks_dev, dtype=jnp.int32)
    near = (jnp.abs(key_ids[:, None] - query_ids[None, :]) <= 1).astype(jnp.int32)
    lead = (key_ids < count).astype(jnp.int32)
    picks = random_blocks.transpose(1, 0, 2)
    times = jnp.sum((picks[:, None, :, :] == key_ids[None, :, None, None]).astype(jnp.int32), axis=-1)
    times = times + near[None] + lead[None, :, None]
    times = jnp.where((query_ids < count)[None, None, :], 1, times)
    bias = jnp.where(times > 0, jnp.log(jnp.maximum(times, 1).astype(F32)), NEGATIVE)
    return jnp.repeat(bias, BLK, axis=2)


def small_outputs(rows):
    return [rows[24], rows[25], rows[16], rows[17], rows[18], rows[8:12].reshape(-1), rows[3], rows[4], rows[5]]


def on_device(
    tokens, cotangent, w_query, b_query, w_key, w_value, b_value, w_out, b_out, first_gain, first_shift,
    w_inner, b_inner, w_outer, b_outer, second_gain, second_shift, global_counts, random_blocks,
):
    _, tok, width = tokens.shape
    ff = w_inner.shape[1]
    blocks_dev = tok // BLK
    shard_count = lax.axis_size("seq")
    shard = lax.axis_index("seq")
    batch = lax.axis_index("batch")
    direct = shard_count == 4 and lax.axis_size("batch") == 8
    if direct:
        core, z = batch & 1, batch >> 1
        x_bit, y_bit = shard & 1, shard >> 1
        first = jnp.where(core == 0, x_bit, y_bit)
        low_z, high_z = z & 1, z >> 1
        mix_0, mix_1 = y_bit * 4 + low_z * 2 + high_z, x_bit * 4 + high_z * 2 + low_z
        info = [core * 2 + first, (1 - core) * 2 + (x_bit + y_bit - first), mix_0, mix_1, core]
        info += [jnp.where(core == 0, mix_0, mix_1), jnp.where(core == 0, mix_1, mix_0)]
        info = jnp.stack(info).astype(jnp.int32)
    else:
        info = jnp.array([0, 2, 0, 0, 0, 0, 0], jnp.int32)
    x = tokens.reshape(tok, width)
    vec = jnp.concatenate(
        [b_query, b_value, b_out, first_gain, first_shift, b_outer, second_gain, second_shift, b_inner]
    ).reshape(-1, width)
    bias = multiplicity_bias(random_blocks[0], global_counts[0], shard, shard_count, blocks_dev)
    pieces = gather_tokens(x, direct)
    rows = tuple(p.shape[0] for p in pieces)
    groups = HEADS // QUAD
    order = Order() if direct else None
    pairs = ((0, 0, 0), (0, 1, 0), (1, 0, 0), (1, 1, 0))
    q, k, v, o, lse = attend(order, pieces, w_query, w_key, w_value, vec, bias)
    layer_out, u1, r1, g_second, g_outer, slope, small_1, hid_t, send_1 = feed(
        order, info, o, x, cotangent.reshape(tok, width), w_out, w_inner, w_outer, vec
    )

    def exchange(value):
        return xor_permute(value, "batch", 1) if direct else value

    got_1 = exchange(send_1)
    keep_1, g_in, low_t, back, small_2, send_2 = inner_back(
        order, info, u1, g_second, g_outer, slope, hid_t, w_inner, w_outer, vec
    )
    if direct:
        one = Unit(order, keep_1, got_1, 2 * width)
        one.step()
    keep_2, g_sum, g_att, dots, small_3, wo_grad = branch_back(order, info, o, u1, r1, back, g_in, low_t, w_out, vec)
    dots = dots[:HEADS].reshape(groups, QUAD, tok)
    got_2 = exchange(send_2)

    def attend_step():
        return attend_back(order, q, k, v, g_att, bias, lse, dots)

    def weights_step():
        return weights(order, info, *backs, wo_grad, pieces, smalls)

    def token_step(starts):
        return token_parts(order, starts, info, *backs, w_query, w_key, w_value, g_sum)

    smalls = (small_1, small_2, small_3)
    if direct:
        two = Unit(order, keep_2, got_2, 2 * width)
        two.step()
        backs = attend_step()
        one.step()
        keep_3, send_3 = weights_step()
        three = Unit(order, keep_3, exchange(send_3), 2 * width)
        two.step()
        one.step()
        parts = token_step((((1, 1), (3, 0)), ((2, -1),)))
        got_a = swap(parts[1], 0)
        two.step()
        one.step()
        three.step()
        two.step()
        one.step()
        (relay,) = combine(order, tok, [[(parts[2], 0), (got_a, 1)]])
        got_b = swap(relay, 1)
        two.step()
        one.step()
        three.step()
        token_grad = token_sum(order, parts[0], got_a, got_b)
        two.step()
        one.step()
        three.step()
        two.step()
        one.step()
        three.step()
        two.step()
        three.step()
        three.step()
        one.forward()
        (d_outer,) = unpack(order, "rows", info, one.held + one.others, pairs, width, ff)
        three.step()
        first = swap(three.held[0], 0)
        two.forward()
        (d_inner,) = unpack(order, "cols", info, two.held + two.others, pairs, width, ff)
        vectors = small_outputs(three.extra)
        three.held[1], vectors, _ = lax.optimization_barrier((three.held[1], vectors, order.last))
        second = swap(three.held[1], 0)
        near = three.held + [exchange(a) for a in three.held]
        made = unpack(order, "four", info, near, ((0, 0, 0), (0, 0, 1), (1, 0, 0), (1, 0, 1)), width, ff)
        far = [first, exchange(first)]
        made = unpack(order, "four", info, far, ((0, 1, 0), (1, 1, 0)), width, ff, made)
        second, made = lax.optimization_barrier((second, made))
        made = unpack(order, "four", info, [second], ((0, 1, 1),), width, ff, made)
        last = unpack(order, "four", info, [exchange(second)], ((1, 1, 1),), width, ff, made)
        d_out, d_query, d_key, d_value = last
    else:
        backs = attend_step()
        keep_3, send_3 = weights_step()
        parts = token_step(tuple(((i, 0),) for i in range(1, shard_count)))
        vectors = small_outputs(lax.psum(keep_3[2 * width :].astype(F32), ("batch", "seq")))
        third = (keep_3[: 2 * width], send_3[: 2 * width])
        d_outer, d_inner, d_four, got = summed_plain(
            info, (keep_1, send_1), (keep_2, send_2), third, parts[1:], width, ff
        )
        (d_outer,), (d_inner,) = d_outer, d_inner
        d_out, d_query, d_key, d_value = d_four
        token_grad = sum([g.astype(F32) for g in got], parts[0])
    return (
        layer_out.reshape(1, tok, width),
        token_grad.reshape(1, tok, width),
        d_query,
        vectors[0],
        d_key,
        d_value,
        vectors[1],
        d_out,
        vectors[2],
        vectors[3],
        vectors[4],
        d_inner,
        vectors[5],
        d_outer,
        vectors[6],
        vectors[7],
        vectors[8],
    )


def solution(mesh):
    token_spec = P("batch", "seq", None)
    placed = (token_spec, token_spec) + (P(),) * 15 + (P("batch"), P("batch", "seq", None, None))
    return jax.shard_map(
        on_device,
        mesh=mesh,
        in_specs=placed,
        out_specs=(token_spec, token_spec) + (P(),) * 15,
        check_vma=False,
    )
```

```python
import functools
import math

import jax
import jax.numpy as jnp
from jax import lax
from jax.experimental import pallas as pl
from jax.experimental.pallas import tpu as pltpu
from jax.sharding import PartitionSpec as P

HEADS = 12
HD = 64
BLK = 64
GMAX = 4
QUAD = 4
EPSILON = 1e-06
NEGATIVE = -1e30
BF = jnp.bfloat16
F32 = jnp.float32
VMEM_BYTES = 24 * 1024 * 1024
EVENT_FLOPS = 43 * 10**6
BACK_FLOPS = 5 * 10**7

NN = (((1,), (0,)), ((), ()))
NT = (((1,), (1,)), ((), ()))
TN = (((0,), (0,)), ((), ()))


def mm(a, b, dims=NN):
    return lax.dot_general(a, b, dims, preferred_element_type=F32)


def params(**kw):
    return pltpu.CompilerParams(vmem_limit_bytes=VMEM_BYTES, **kw)


def cost(flops, bytes_accessed, exps=0):
    return pl.CostEstimate(flops=flops * 100, bytes_accessed=bytes_accessed * 100, transcendentals=exps * 100)


def ordered(body, order, in_specs, args, name, out_specs, out_shape, **kw):
    if order is None:
        return pl.pallas_call(
            body, in_specs=in_specs, out_specs=out_specs, out_shape=out_shape, name=name, **kw
        )(*args)
    one = not isinstance(out_shape, (list, tuple))
    specs, shapes = ([out_specs], [out_shape]) if one else (list(out_specs), list(out_shape))
    marks = [] if order.last is None else [order.last]
    n, made = len(args), len(shapes)
    mark = jax.ShapeDtypeStruct((8, 128), F32)

    def kernel(*refs):
        outs = refs[n + len(marks) :]
        outs[made][...] = jnp.zeros_like(outs[made])
        body(*refs[:n], *outs[:made], *outs[made + 1 :])

    mark_spec = pl.BlockSpec((8, 128), lambda *_: (0, 0))
    *out, order.last = pl.pallas_call(
        kernel,
        in_specs=list(in_specs) + [pl.BlockSpec(memory_space=pl.ANY)] * len(marks),
        out_specs=specs + [mark_spec],
        out_shape=shapes + [mark],
        name=name,
        **kw,
    )(*args, *marks)
    return out[0] if one else out


def whole(shape):
    return pl.BlockSpec(shape, lambda *_: (0,) * len(shape))


def half_mask(values, side):
    lane = lax.broadcasted_iota(jnp.int32, values.shape, 1)
    keep = lane < HD if side == 0 else lane >= HD
    return jnp.where(keep, values, jnp.zeros_like(values))


def attend_body(rows, *refs):
    n = len(rows)
    pieces = refs[:n]
    wq, wk, wv, vec, bias = refs[n : n + 5]
    q_out, k_out, v_out, o_out, lse_out = refs[n + 5 : n + 10]
    vt, sc, ot = refs[n + 10 :]
    q = (mm(pieces[0][...], wq[...]) + vec[0:1, :]).astype(BF)
    q_out[...] = (q.astype(F32) * (1.0 / math.sqrt(HD))).astype(BF)
    start = 0
    for piece, count in zip(pieces, rows):
        x = piece[...]
        k_out[0, start : start + count, :] = mm(x, wk[...]).astype(BF)
        v = mm(x, wv[...]) + vec[1:2, :]
        v_out[0, start : start + count, :] = v.astype(BF)
        vt[:, start : start + count] = v.astype(BF).T
        start += count
    total = start
    step = 256
    per = step // BLK
    for head in range(QUAD):
        lanes = slice(head // 2 * 128, head // 2 * 128 + 128)
        qh = half_mask(q_out[:, lanes], head % 2)
        top = jnp.full((1, qh.shape[0]), NEGATIVE, F32)
        for c in range(total // step):
            part = mm(k_out[0, c * step : (c + 1) * step, lanes], qh, NT)
            for b in range(per):
                row = bias[head, c * per + b : c * per + b + 1, :]
                s = part[b * BLK : (b + 1) * BLK, :] + row
                sc[c * step + b * BLK : c * step + (b + 1) * BLK, :] = s
                top = jnp.maximum(top, jnp.max(s, axis=0, keepdims=True))
        acc = jnp.zeros((HD, qh.shape[0]), F32)
        norm = jnp.zeros((1, qh.shape[0]), F32)
        for c in range(total // step):
            e = jnp.exp(sc[c * step : (c + 1) * step, :] - top)
            norm = norm + jnp.sum(e, axis=0, keepdims=True)
            acc = acc + mm(vt[head * HD : (head + 1) * HD, c * step : (c + 1) * step], e.astype(BF))
        ot[head * HD : (head + 1) * HD, :] = acc / norm
        lse_out[0, head : head + 1, :] = top + jnp.log(norm)
    o_out[...] = ot[...].T


def attend(order, pieces, wq, wk, wv, vec, bias):
    rows = tuple(p.shape[0] for p in pieces)
    total = sum(rows)
    tok, width = pieces[0].shape
    groups = HEADS // QUAD
    cols = QUAD * HD
    col = lambda r: pl.BlockSpec((r, cols), lambda g: (0, g))
    return ordered(
        functools.partial(attend_body, rows),
        order,
        [whole((r, width)) for r in rows]
        + [col(width), col(width), col(width), col(vec.shape[0])]
        + [pl.BlockSpec((QUAD,) + bias.shape[1:], lambda g: (g, 0, 0))],
        (*pieces, *(pltpu.with_memory_space_constraint(w, pltpu.HBM) for w in (wq, wk, wv)), vec, bias),
        "attend",
        grid=(groups,),
        out_specs=[
            col(tok),
            pl.BlockSpec((1, total, cols), lambda g: (g, 0, 0)),
            pl.BlockSpec((1, total, cols), lambda g: (g, 0, 0)),
            col(tok),
            pl.BlockSpec((1, QUAD, tok), lambda g: (g, 0, 0)),
        ],
        out_shape=[
            pltpu.HBM((tok, width), BF),
            pltpu.HBM((groups, total, cols), BF),
            pltpu.HBM((groups, total, cols), BF),
            jax.ShapeDtypeStruct((tok, width), F32),
            jax.ShapeDtypeStruct((groups, QUAD, tok), F32),
        ],
        scratch_shapes=[
            pltpu.VMEM((cols, total), BF),
            pltpu.VMEM((total, tok), F32),
            pltpu.VMEM((cols, tok), F32),
        ],
        cost_estimate=cost(2 * total * 256 * (2 * HEADS * tok + 3 * width * 2), 4 * total * width * 2, HEADS * tok * total),
        compiler_params=params(),
    )


def norm_stats(values):
    mean = jnp.mean(values, axis=-1, keepdims=True)
    centred = values - mean
    r = lax.rsqrt(jnp.mean(centred * centred, axis=-1, keepdims=True) + EPSILON)
    return centred * r, r


def norm_back(e, u, r):
    return r * (e - jnp.mean(e, axis=-1, keepdims=True) - u * jnp.mean(e * u, axis=-1, keepdims=True))


def colsum(values):
    return jnp.sum(values, axis=0, keepdims=True)


def put_pieces(dst, base, block, mix, size=96):
    for p in range(block.shape[0] // size):
        at = pl.multiple_of(base + (p ^ mix) * size, 16)
        dst[pl.ds(at, size), :] = block[p * size : (p + 1) * size, :]


def feed_body(
    info, o_in, x_in, cot_in, wo, wi, wu, vec,
    layer_out, u1_out, r1_out, g_second_out, g_outer_out, slope, small_out, hid_t, send,
):
    small_out[...] = jnp.zeros_like(small_out)
    width = wo.shape[0]
    chunks = wi.shape[1] // width
    b_out, fg, fs, b_outer, sg, ss = (vec[i : i + 1, :] for i in range(2, 8))
    att = o_in[...].astype(BF)
    first_in = x_in[...].astype(F32) + (mm(att, wo[...]) + b_out)
    u1, r1 = norm_stats(first_in)
    u1_out[...] = u1
    r1_out[...] = jnp.broadcast_to(r1, r1_out.shape)
    first = u1 * fg + fs
    low = first.astype(BF)
    out = jnp.zeros_like(first)
    for j in range(chunks):
        cols = slice(j * width, (j + 1) * width)
        v = mm(low, wi[:, cols]) + vec[8 + j : 9 + j, :]
        t = jnp.tanh(0.7978845608028654 * (v + 0.044715 * v * v * v))
        h = 0.5 * v * (1.0 + t)
        slope[:, cols] = 0.5 * (1.0 + t) + 0.5 * v * (1.0 - t * t) * (
            0.7978845608028654 * (1.0 + 3.0 * 0.044715 * v * v)
        )
        out = out + mm(h.astype(BF), wu[cols, :])
        put_pieces(hid_t, j * width, h.astype(BF).T, info[2 + 2 * j // chunks])
    u2, r2 = norm_stats(first + (out + b_outer))
    layer_out[...] = (u2 * sg + ss).astype(BF)
    cot = cot_in[...].astype(F32)
    small_out[4:5, :] = colsum(cot * u2)
    small_out[5:6, :] = colsum(cot)
    g_second = norm_back(cot * sg, u2, r2)
    g_second_out[...] = g_second
    g_outer = g_second.astype(BF)
    g_outer_out[...] = g_outer
    small_out[3:4, :] = colsum(g_outer.astype(F32))
    for j in range(chunks // 2):
        at = pl.multiple_of((j ^ info[1]) * width, width)
        send[j * width : (j + 1) * width, :] = mm(hid_t[pl.ds(at, width), :], g_outer).astype(BF)


VM = pl.BlockSpec(memory_space=pltpu.VMEM)
SM = pl.BlockSpec(memory_space=pltpu.SMEM)
ANYWHERE = pl.BlockSpec(memory_space=pl.ANY)


def feed(order, info, o, x, cot, wo, wi, wu, vec):
    tok, width = x.shape
    ff = wi.shape[1]
    return ordered(
        feed_body,
        order,
        [SM] + [VM] * 7,
        (info, o, x, cot, wo, wi, wu, vec,),
        "feed",
        out_specs=[VM] * 9,
        out_shape=[
            jax.ShapeDtypeStruct((tok, width), BF),
            jax.ShapeDtypeStruct((tok, width), F32),
            jax.ShapeDtypeStruct((tok, 128), F32),
            jax.ShapeDtypeStruct((tok, width), F32),
            jax.ShapeDtypeStruct((tok, width), BF),
            jax.ShapeDtypeStruct((tok, ff), F32),
            jax.ShapeDtypeStruct((8, width), F32),
            jax.ShapeDtypeStruct((ff, tok), BF),
            pltpu.HBM((ff // 2, width), BF),
        ],
        cost_estimate=cost(2 * tok * width * (5 * ff // 2 + width), 4 * (width * ff * 2), tok * ff),
        compiler_params=params(),
    )


def inner_back_body(
    info, u1_in, g_second_in, g_outer_in, slope, hid_t, wi, wu, vec,
    keep, g_in, low_t, back_out, small_out, send,
):
    small_out[...] = jnp.zeros_like(small_out)
    width = wi.shape[0]
    chunks = wi.shape[1] // width
    g_outer = g_outer_in[...]
    for j in range(chunks // 2):
        at = pl.multiple_of((j ^ info[0]) * width, width)
        keep[j * width : (j + 1) * width, :] = mm(hid_t[pl.ds(at, width), :], g_outer).astype(BF)
    flat_t = (u1_in[...] * vec[3:4, :] + vec[4:5, :]).astype(BF).T
    for c in range(2):
        put_pieces(low_t.at[c], 0, flat_t, info[2 + c])
    back = g_second_in[...]
    for j in range(chunks):
        cols = slice(j * width, (j + 1) * width)
        gi = (mm(g_outer, wu[cols, :], NT) * slope[:, cols]).astype(BF)
        g_in[:, cols] = gi
        small_out[j : j + 1, :] = colsum(gi.astype(F32))
        back = back + mm(gi, wi[:, cols], NT)
    back_out[...] = back
    for j in range(chunks // 2):
        at = pl.multiple_of((j ^ info[1]) * width, width)
        send[j * width : (j + 1) * width, :] = mm(low_t[1 - info[4]], g_in[:, pl.ds(at, width)]).astype(BF)


def inner_back(order, info, u1, g_second, g_outer, slope, hid_t, wi, wu, vec):
    tok, width = u1.shape
    ff = wi.shape[1]
    half = pltpu.HBM((ff // 2, width), BF)
    return ordered(
        inner_back_body,
        order,
        [SM] + [VM] * 8,
        (info, u1, g_second, g_outer, slope, hid_t, wi, wu, vec,),
        "inner_back",
        out_specs=[VM] * 6,
        out_shape=[
            half,
            jax.ShapeDtypeStruct((tok, ff), BF),
            jax.ShapeDtypeStruct((2, width, tok), BF),
            jax.ShapeDtypeStruct((tok, width), F32),
            jax.ShapeDtypeStruct((8, width), F32),
            half,
        ],
        cost_estimate=cost(2 * tok * width * 3 * ff, 4 * (width * ff * 2)),
        compiler_params=params(),
    )


def branch_back_body(
    info, o_in, u1_in, r1_in, back_in, g_in, low_t, wo_in, vec,
    keep, g_sum_out, g_att_out, dots_out, small_out, wo_a,
    att_t,
):
    small_out[...] = jnp.zeros_like(small_out)
    width = wo_in.shape[0]
    for j in range(keep.shape[0] // width):
        at = pl.multiple_of((j ^ info[0]) * width, width)
        keep[j * width : (j + 1) * width, :] = mm(low_t[info[4]], g_in[:, pl.ds(at, width)]).astype(BF)
    back, u1 = back_in[...], u1_in[...]
    small_out[1:2, :] = colsum(back * u1)
    small_out[2:3, :] = colsum(back)
    g_sum = norm_back(back * vec[3:4, :], u1, r1_in[:, 0:1])
    g_sum_out[...] = g_sum
    g_branch = g_sum.astype(BF)
    small_out[0:1, :] = colsum(g_branch.astype(F32))
    o = o_in[...]
    g_att = mm(g_branch, wo_in[...], NT).astype(BF)
    g_att_out[...] = g_att
    put_pieces(att_t, 0, o.astype(BF).T, info[2])
    wo_a[...] = mm(att_t[...], g_branch).astype(BF)
    head = lax.broadcasted_iota(jnp.int32, (16, width), 0)
    lane = lax.broadcasted_iota(jnp.int32, (16, width), 1)
    pick = jnp.where(lane // HD == head, 1.0, 0.0).astype(F32)
    dots_out[...] = lax.dot_general(
        pick, g_att.astype(F32) * o, NT, precision=lax.Precision.HIGHEST, preferred_element_type=F32
    )


def branch_back(order, info, o, u1, r1, back, g_in, low_t, wo, vec):
    tok, width = o.shape
    ff = g_in.shape[1]
    return ordered(
        branch_back_body,
        order,
        [SM] + [VM] * 8,
        (info, o, u1, r1, back, g_in, low_t, wo, vec,),
        "branch_back",
        out_specs=[VM] * 6,
        out_shape=[
            pltpu.HBM((ff // 2, width), BF),
            pltpu.HBM((tok, width), F32),
            pltpu.HBM((tok, width), BF),
            jax.ShapeDtypeStruct((16, tok), F32),
            jax.ShapeDtypeStruct((8, width), F32),
            pltpu.HBM((width, width), BF),
        ],
        scratch_shapes=[pltpu.VMEM((width, tok), BF)],
        cost_estimate=cost(2 * tok * width * (ff // 2 + 2 * width), 4 * width * ff),
        compiler_params=params(),
    )


def attend_back_body(q_in, k_in, v_in, g_in, bias, lse, dots, dq_out, dk_out, dv_out, kt, dqt):
    total = k_in.shape[1]
    step = 256
    per = step // BLK
    kt[...] = k_in[0].T
    for pair in range(QUAD // 2):
        lanes = slice(pair * 128, pair * 128 + 128)
        qs = [half_mask(q_in[:, lanes], s) for s in range(2)]
        gs = [half_mask(g_in[:, lanes], s) for s in range(2)]
        dqs = [jnp.zeros((HD, q_in.shape[0]), F32) for _ in range(2)]
        for c in range(total // step):
            rows = slice(c * step, (c + 1) * step)
            kc = k_in[0, rows, lanes]
            vc = v_in[0, rows, lanes]
            dk = jnp.zeros((step, 128), F32)
            dv = jnp.zeros((step, 128), F32)
            for s in range(2):
                head = pair * 2 + s
                sc = mm(kc, qs[s], NT)
                dp = mm(vc, gs[s], NT)
                shift = bias[head, c * per : (c + 1) * per, :] - lse[0, head : head + 1, :]
                p = jnp.concatenate(
                    [jnp.exp(sc[b * BLK : (b + 1) * BLK, :] + shift[b : b + 1, :]) for b in range(per)], axis=0
                )
                ds = (p * (dp - dots[0, head : head + 1, :])).astype(BF)
                dv = dv + mm(p.astype(BF), gs[s])
                dk = dk + mm(ds, qs[s])
                dqs[s] = dqs[s] + mm(kt[head * HD : (head + 1) * HD, rows], ds)
            dk_out[0, rows, lanes] = dk.astype(BF)
            dv_out[0, rows, lanes] = dv.astype(BF)
        for s in range(2):
            head = pair * 2 + s
            dqt[head * HD : (head + 1) * HD, :] = dqs[s]
    dq_out[0] = (dqt[...].T * (1.0 / math.sqrt(HD))).astype(BF)


def attend_back(order, q, k, v, g, bias, lse, dots):
    tok, width = q.shape
    groups, total, cols = k.shape
    col = pl.BlockSpec((tok, cols), lambda i: (0, i))
    group = lambda r: pl.BlockSpec((1, r, cols), lambda i: (i, 0, 0))
    stat = pl.BlockSpec((1, QUAD, tok), lambda i: (i, 0, 0))
    return ordered(
        attend_back_body,
        order,
        [col, group(total), group(total), col]
        + [pl.BlockSpec((QUAD,) + bias.shape[1:], lambda i: (i, 0, 0)), stat, stat],
        (*(pltpu.with_memory_space_constraint(a, pltpu.HBM) for a in (q, k, v, g)), bias, lse, dots),
        "attend_back",
        grid=(groups,),
        out_specs=[group(tok), group(total), group(total)],
        out_shape=[jax.ShapeDtypeStruct((groups, r, cols), BF) for r in (tok, total, total)],
        scratch_shapes=[pltpu.VMEM((cols, total), BF), pltpu.VMEM((cols, tok), F32)],
        cost_estimate=cost(BACK_FLOPS, 1 << 20),
        compiler_params=params(),
    )


def weights_body(rows, smalls, info, wo_grad, *refs):
    n = len(rows)
    small_in, refs = refs[:smalls], refs[smalls:]
    groups = HEADS // QUAD
    dqs, dks, dvs = refs[:3]
    pieces = refs[3 : 3 + n]
    keep, send = refs[3 + n : 5 + n]
    x0, x1, tmp, small = refs[5 + n :]
    own = rows[0]
    start = 0
    for piece, count in zip(pieces, rows):
        t = piece[...].T
        for p in range(t.shape[0] // 96):
            for xt, mix in ((x0, info[2]), (x1, info[3])):
                if start < own or xt is x1:
                    at = pl.multiple_of((p ^ mix) * 96, 16)
                    xt[pl.ds(at, 96), start : start + count] = t[p * 96 : (p + 1) * 96, :]
        start += count
    small[...] = jnp.zeros_like(small)
    cols = QUAD * HD
    width = keep.shape[1]
    for g in range(groups):
        lanes = slice(g * cols, (g + 1) * cols)
        small[0:1, lanes] = colsum(dqs[g].astype(F32))
        small[1:2, lanes] = colsum(dvs[g].astype(F32))
        tmp[0] = wo_grad[:, lanes]
        tmp[1] = mm(x0[...], dqs[g]).astype(BF)
        tmp[2] = mm(x1[...], dks[g]).astype(BF)
        tmp[3] = mm(x1[...], dvs[g]).astype(BF)
        for j in range(2):
            keep[j * width : (j + 1) * width, lanes] = tmp[j ^ info[0]]
            send[j * width : (j + 1) * width, lanes] = tmp[j ^ info[1]]
    tail = jnp.concatenate([r[...] for r in small_in] + [small[...]], axis=0).astype(BF)
    keep[2 * width :, :] = tail
    send[2 * width :, :] = tail


def weights(order, info, dqs, dks, dvs, wo_grad, pieces, smalls):
    rows = tuple(p.shape[0] for p in pieces)
    total = sum(rows)
    width = wo_grad.shape[0]
    _, tok, cols = dqs.shape
    half = pltpu.HBM((2 * width + 8 * (len(smalls) + 1), width), BF)
    count = 1 + len(smalls) + 3 + len(rows)
    return ordered(
        functools.partial(weights_body, rows, len(smalls)),
        order,
        [SM] + [VM] * count,
        (info, wo_grad, *smalls, dqs, dks, dvs, *pieces),
        "weights",
        out_specs=[VM] * 2,
        out_shape=[half, half],
        scratch_shapes=[
            pltpu.VMEM((width, tok), BF),
            pltpu.VMEM((width, total), BF),
            pltpu.VMEM((4, width, cols), BF),
            pltpu.VMEM((8, width), F32),
        ],
        cost_estimate=cost(2 * width * width * (tok + 2 * total), 4 * width * width * 4),
        compiler_params=params(),
    )


def token_body(starts, count, info, wq, wk, wv, g_sum, *refs):
    groups = HEADS // QUAD
    dqs, dks, dvs = refs[:3]
    own, outs = refs[3], refs[4:]
    cols = QUAD * HD

    def part(place):
        rows = pl.ds(place * count if isinstance(place, int) else pl.multiple_of(place * count, count), count)
        t = jnp.zeros((count, wq.shape[0]), F32)
        for g in range(groups):
            lanes = slice(g * cols, (g + 1) * cols)
            t = t + mm(dks[g, rows, :], wk[:, lanes], NT)
            t = t + mm(dvs[g, rows, :], wv[:, lanes], NT)
        return t

    t = part(0) + g_sum[...]
    for g in range(groups):
        t = t + mm(dqs[g], wq[:, g * cols : (g + 1) * cols], NT)
    own[...] = t
    for out, places in zip(outs, starts):
        for i, (base, sign) in enumerate(places):
            place = base if sign == 0 else base + sign * info[4]
            out[i * count : (i + 1) * count, :] = part(place).astype(BF)


def token_parts(order, starts, info, dqs, dks, dvs, wq, wk, wv, g_sum):
    tok, width = g_sum.shape
    return ordered(
        functools.partial(token_body, starts, tok),
        order,
        [SM] + [VM] * (4 + 3),
        (info, wq, wk, wv, g_sum, dqs, dks, dvs),
        "token_parts",
        out_specs=[VM] * (1 + len(starts)),
        out_shape=[jax.ShapeDtypeStruct((tok, width), F32)]
        + [jax.ShapeDtypeStruct((tok * len(p), width), BF) for p in starts],
        cost_estimate=cost(2 * width * width * 9 * tok, 4 * width * width * 4),
        compiler_params=params(),
    )


def unpack_body(kind, blocks, made, info, *refs):
    n = len(blocks)
    ins = refs[:n]
    refs = refs[n + made :]
    count = len(refs) - 2
    outs, wide, sems = refs[:count], refs[count], refs[count + 1]
    size = 96
    rows, width = ins[0].shape
    pieces = rows // size
    copies = []
    for b, (ref, (side, j, half)) in enumerate(zip(ins, blocks)):
        mix = info[5 + side]
        for i in range(pieces):
            at = pl.multiple_of((i ^ (mix & (pieces - 1))) * size, 32)
            wide[b, pl.ds(at, size), :] = ref[i * size : (i + 1) * size, :].astype(F32)
        chunk = info[side] ^ j
        if kind == "four":
            at = pl.multiple_of((half ^ (mix // pieces)) * rows, rows)
            targets = [(chunk == c, outs[c].at[pl.ds(at, rows), :]) for c in range(4)]
        else:
            at = pl.multiple_of(chunk * width, width)
            targets = [(None, outs[0].at[pl.ds(at, width), :] if kind == "rows" else outs[0].at[:, pl.ds(at, width)])]
        for when, out in targets:
            copy = pltpu.make_async_copy(wide.at[b], out, sems.at[b])
            copies.append((when, copy))
            if when is None:
                copy.start()
            else:
                pl.when(when)(copy.start)
    for when, copy in copies:
        if when is None:
            copy.wait()
        else:
            pl.when(when)(copy.wait)


def unpack(order, kind, info, arrays, blocks, width, ff, made=()):
    shapes = {
        "rows": [(ff, width)],
        "cols": [(width, ff)],
        "four": [(width, width)] * 4,
    }[kind]
    return ordered(
        functools.partial(unpack_body, kind, blocks, len(made)),
        order,
        [SM] + [VM] * len(arrays) + [ANYWHERE] * len(made),
        (info, *arrays, *made),
        "unpack_" + kind,
        out_specs=[ANYWHERE] * len(shapes),
        out_shape=[jax.ShapeDtypeStruct(s, F32) for s in shapes],
        scratch_shapes=[
            pltpu.VMEM((len(arrays),) + arrays[0].shape, F32),
            pltpu.SemaphoreType.DMA((len(arrays),)),
        ],
        input_output_aliases={1 + len(arrays) + i: i for i in range(len(made))},
        cost_estimate=cost(ff * width, 6 * ff * width),
        compiler_params=params(),
    )


def xor_permute(value, axis, mask):
    size = lax.axis_size(axis)
    return lax.ppermute(value, axis, [(i, i ^ mask) for i in range(size)])


def rows_at(count, index):
    return pl.BlockSpec((count, 768), lambda *_: (index, 0))


def in_hbm(array):
    return pltpu.with_memory_space_constraint(array, pltpu.HBM) if array.shape[0] > 1024 else array


def combine_body(ways, terms, extras, *refs):
    ins, outs = refs[: ways * terms + extras], refs[ways * terms + extras :]
    for w in range(ways):
        value = ins[w * terms][...].astype(F32)
        for r in ins[w * terms + 1 : (w + 1) * terms]:
            value = value + r[...].astype(F32)
        outs[w][: value.shape[0], :] = value.astype(BF)
    if extras:
        tail = (ins[ways * terms][...].astype(F32) + ins[ways * terms + 1][...].astype(F32)).astype(BF)
        for out in outs:
            out[out.shape[0] - tail.shape[0] :, :] = tail


def combine(order, count, ways, extras=()):
    width = ways[0][0][0].shape[1]
    terms = [t for way in ways for t in way]
    made = jax.ShapeDtypeStruct((count + (32 if extras else 0), width), BF)
    steps = 1 if extras or count < 384 else 2
    part = count // steps

    def at(index):
        return pl.BlockSpec((part, width), lambda i: (index * steps + i, 0))

    return ordered(
        functools.partial(combine_body, len(ways), len(ways[0]), len(extras)),
        order,
        [at(i) for _, i in terms] + [rows_at(32, i) for _, i in extras],
        (*(in_hbm(a) for a, _ in terms), *(in_hbm(a) for a, _ in extras)),
        "combine",
        grid=(steps,),
        out_specs=[pl.BlockSpec((made.shape[0] // steps, width), lambda i: (i, 0))] * len(ways),
        out_shape=[made] * len(ways),
        cost_estimate=cost(EVENT_FLOPS, 1 << 20),
        compiler_params=params(),
    )


def finish_body(parts, extras, *refs):
    ins, outs = refs[: parts + extras], refs[parts + extras :]
    value = ins[0][...].astype(F32)
    for r in ins[1:parts]:
        value = value + r[...].astype(F32)
    outs[0][...] = value.astype(BF)
    if extras:
        outs[1][...] = ins[parts][...].astype(F32) + ins[parts + 1][...].astype(F32)


def finish(order, arrays, count, extras=()):
    width = arrays[0].shape[1]
    out = [jax.ShapeDtypeStruct((count, width), BF)]
    if extras:
        out.append(jax.ShapeDtypeStruct((32, width), F32))
    return ordered(
        functools.partial(finish_body, len(arrays), len(extras)),
        order,
        [rows_at(count, 0)] * len(arrays) + [rows_at(32, i) for _, i in extras],
        (*(in_hbm(a) for a in arrays), *(in_hbm(a) for a, _ in extras)),
        "finish",
        grid=(1,),
        out_specs=[pl.BlockSpec(o.shape, lambda *_: (0, 0)) for o in out],
        out_shape=out,
        cost_estimate=cost(EVENT_FLOPS, 1 << 20),
        compiler_params=params(),
    )


def token_sum_body(own, first, second, out):
    out[...] = own[...] + (first[...].astype(F32) + second[...].astype(F32))


def token_sum(order, own, first, second):
    tok, width = own.shape
    block = pl.BlockSpec((tok, width), lambda *_: (0, 0))
    return ordered(
        token_sum_body,
        order,
        [block] * 3,
        (own, first, second),
        "token_sum",
        grid=(1,),
        out_specs=block,
        out_shape=jax.ShapeDtypeStruct((tok, width), F32),
        cost_estimate=cost(EVENT_FLOPS, 1 << 20),
        compiler_params=params(),
    )


def stack_body(*refs):
    at = 0
    for r in refs[:-1]:
        refs[-1][at : at + r.shape[0], :] = r[...]
        at += r.shape[0]


def stack(order, arrays):
    rows, width = sum(a.shape[0] for a in arrays), arrays[0].shape[1]
    return ordered(
        stack_body,
        order,
        [VM] * len(arrays),
        (*arrays,),
        "stack",
        out_specs=VM,
        out_shape=jax.ShapeDtypeStruct((rows, width), arrays[0].dtype),
        cost_estimate=cost(EVENT_FLOPS, 1 << 20),
        compiler_params=params(),
    )


STAGES = (((1, 0), (2, 0)), ((2, 0), (1, 0)), ((0, 2), (0, 4)), ((0, 4), (0, 2)))


def swap(value, stage):
    shards = lax.axis_size("seq")
    pairs = []
    for b in range(lax.axis_size("batch")):
        of_shard, of_batch = STAGES[stage][b % 2]
        pairs += [(b * shards + s, (b ^ of_batch) * shards + (s ^ of_shard)) for s in range(shards)]
    return lax.ppermute(value, ("batch", "seq"), pairs)


class Order:
    def __init__(self):
        self.last = None


class Unit:
    def __init__(self, order, keep, got, rows):
        self.order, self.rows, self.stage = order, rows, 0
        self.parts = [keep, got]
        self.extra = [(a, rows // 32) for a in self.parts] if keep.shape[0] > rows else []

    def step(self):
        if self.stage < 4:
            half = self.rows // 2
            (sent,) = combine(self.order, half, [[(p, 1) for p in self.parts]], self.extra)
            got = swap(sent, self.stage)
            if self.extra:
                self.extra = [(sent, half // 32), (got, half // 32)]
            self.parts.append(got)
            self.rows = half
        else:
            if self.stage == 4:
                body, *tail = finish(self.order, self.parts, self.rows, self.extra)
                self.extra = tail[0] if tail else None
            else:
                body = stack(self.order, self.held)
            self.held = [body, swap(body, 7 - self.stage)]
        self.stage += 1

    def forward(self):
        self.others = [xor_permute(a, "batch", 1) for a in self.held]


def summed_plain(info, first, second, third, tokens, width, ff):
    axes = ("batch", "seq")

    def whole_sum(keep, send):
        part = lax.psum_scatter(jnp.concatenate([keep, send], axis=0), axes, scatter_dimension=0, tiled=True)
        return lax.all_gather(part, axes, axis=0, tiled=True)

    blocks = ((0, 0, 0), (0, 1, 0), (1, 0, 0), (1, 1, 0))

    def placed(kind, pair):
        total = whole_sum(*pair)
        return unpack(None, kind, info, [total[i * width : (i + 1) * width] for i in range(4)], blocks, width, ff)

    d_outer = placed("rows", first)
    d_inner = placed("cols", second)
    d_four = placed("four", third)
    return d_outer, d_inner, d_four, [xor_permute(t, "seq", k) for k, t in enumerate(tokens, 1)]


def gather_tokens(x, small):
    size = lax.axis_size("seq")
    if small:
        a = xor_permute(x, "seq", 1)
        b = xor_permute(x, "seq", 2)
        half = x.shape[0] // 2
        return [x, a, b, xor_permute(a[:half], "seq", 2), xor_permute(b[half:], "seq", 1)]
    return [x] + [xor_permute(x, "seq", k) for k in range(1, size)]


def multiplicity_bias(random_blocks, count, shard_index, shard_count, blocks_dev):
    order = shard_index ^ jnp.arange(shard_count, dtype=jnp.int32)
    key_ids = (order[:, None] * blocks_dev + jnp.arange(blocks_dev, dtype=jnp.int32)[None, :]).reshape(-1)
    query_ids = shard_index * blocks_dev + jnp.arange(blocks_dev, dtype=jnp.int32)
    near = (jnp.abs(key_ids[:, None] - query_ids[None, :]) <= 1).astype(jnp.int32)
    lead = (key_ids < count).astype(jnp.int32)
    picks = random_blocks.transpose(1, 0, 2)
    times = jnp.sum((picks[:, None, :, :] == key_ids[None, :, None, None]).astype(jnp.int32), axis=-1)
    times = times + near[None] + lead[None, :, None]
    times = jnp.where((query_ids < count)[None, None, :], 1, times)
    bias = jnp.where(times > 0, jnp.log(jnp.maximum(times, 1).astype(F32)), NEGATIVE)
    return jnp.repeat(bias, BLK, axis=2)


def small_outputs(rows):
    return [rows[24], rows[25], rows[16], rows[17], rows[18], rows[8:12].reshape(-1), rows[3], rows[4], rows[5]]


def on_device(
    tokens, cotangent, w_query, b_query, w_key, w_value, b_value, w_out, b_out, first_gain, first_shift,
    w_inner, b_inner, w_outer, b_outer, second_gain, second_shift, global_counts, random_blocks,
):
    _, tok, width = tokens.shape
    ff = w_inner.shape[1]
    blocks_dev = tok // BLK
    shard_count = lax.axis_size("seq")
    shard = lax.axis_index("seq")
    batch = lax.axis_index("batch")
    direct = shard_count == 4 and lax.axis_size("batch") == 8
    if direct:
        core, z = batch & 1, batch >> 1
        x_bit, y_bit = shard & 1, shard >> 1
        first = jnp.where(core == 0, x_bit, y_bit)
        low_z, high_z = z & 1, z >> 1
        mix_0, mix_1 = y_bit * 4 + low_z * 2 + high_z, x_bit * 4 + high_z * 2 + low_z
        info = [core * 2 + first, (1 - core) * 2 + (x_bit + y_bit - first), mix_0, mix_1, core]
        info += [jnp.where(core == 0, mix_0, mix_1), jnp.where(core == 0, mix_1, mix_0)]
        info = jnp.stack(info).astype(jnp.int32)
    else:
        info = jnp.array([0, 2, 0, 0, 0, 0, 0], jnp.int32)
    x = tokens.reshape(tok, width)
    vec = jnp.concatenate(
        [b_query, b_value, b_out, first_gain, first_shift, b_outer, second_gain, second_shift, b_inner]
    ).reshape(-1, width)
    bias = multiplicity_bias(random_blocks[0], global_counts[0], shard, shard_count, blocks_dev)
    pieces = gather_tokens(x, direct)
    rows = tuple(p.shape[0] for p in pieces)
    groups = HEADS // QUAD
    order = Order() if direct else None
    pairs = ((0, 0, 0), (0, 1, 0), (1, 0, 0), (1, 1, 0))
    q, k, v, o, lse = attend(order, pieces, w_query, w_key, w_value, vec, bias)
    layer_out, u1, r1, g_second, g_outer, slope, small_1, hid_t, send_1 = feed(
        order, info, o, x, cotangent.reshape(tok, width), w_out, w_inner, w_outer, vec
    )

    def exchange(value):
        return xor_permute(value, "batch", 1) if direct else value

    got_1 = exchange(send_1)
    keep_1, g_in, low_t, back, small_2, send_2 = inner_back(
        order, info, u1, g_second, g_outer, slope, hid_t, w_inner, w_outer, vec
    )
    if direct:
        one = Unit(order, keep_1, got_1, 2 * width)
        one.step()
    keep_2, g_sum, g_att, dots, small_3, wo_grad = branch_back(order, info, o, u1, r1, back, g_in, low_t, w_out, vec)
    dots = dots[:HEADS].reshape(groups, QUAD, tok)
    got_2 = exchange(send_2)

    def attend_step():
        return attend_back(order, q, k, v, g_att, bias, lse, dots)

    def weights_step():
        return weights(order, info, *backs, wo_grad, pieces, smalls)

    def token_step(starts):
        return token_parts(order, starts, info, *backs, w_query, w_key, w_value, g_sum)

    smalls = (small_1, small_2, small_3)
    if direct:
        two = Unit(order, keep_2, got_2, 2 * width)
        two.step()
        backs = attend_step()
        one.step()
        keep_3, send_3 = weights_step()
        three = Unit(order, keep_3, exchange(send_3), 2 * width)
        two.step()
        one.step()
        parts = token_step((((1, 1), (3, 0)), ((2, -1),)))
        got_a = swap(parts[1], 0)
        two.step()
        one.step()
        three.step()
        two.step()
        one.step()
        (relay,) = combine(order, tok, [[(parts[2], 0), (got_a, 1)]])
        got_b = swap(relay, 1)
        two.step()
        one.step()
        three.step()
        token_grad = token_sum(order, parts[0], got_a, got_b)
        two.step()
        one.step()
        three.step()
        two.step()
        one.step()
        three.step()
        two.step()
        three.step()
        three.step()
        one.forward()
        (d_outer,) = unpack(order, "rows", info, one.held + one.others, pairs, width, ff)
        three.step()
        first = swap(three.held[0], 0)
        two.forward()
        (d_inner,) = unpack(order, "cols", info, two.held + two.others, pairs, width, ff)
        vectors = small_outputs(three.extra)
        three.held[1], vectors, _ = lax.optimization_barrier((three.held[1], vectors, order.last))
        second = swap(three.held[1], 0)
        near = three.held + [exchange(a) for a in three.held]
        made = unpack(order, "four", info, near, ((0, 0, 0), (0, 0, 1), (1, 0, 0), (1, 0, 1)), width, ff)
        far = [first, exchange(first)]
        made = unpack(order, "four", info, far, ((0, 1, 0), (1, 1, 0)), width, ff, made)
        second, made = lax.optimization_barrier((second, made))
        made = unpack(order, "four", info, [second], ((0, 1, 1),), width, ff, made)
        last = unpack(order, "four", info, [exchange(second)], ((1, 1, 1),), width, ff, made)
        d_out, d_query, d_key, d_value = last
    else:
        backs = attend_step()
        keep_3, send_3 = weights_step()
        parts = token_step(tuple(((i, 0),) for i in range(1, shard_count)))
        vectors = small_outputs(lax.psum(keep_3[2 * width :].astype(F32), ("batch", "seq")))
        third = (keep_3[: 2 * width], send_3[: 2 * width])
        d_outer, d_inner, d_four, got = summed_plain(
            info, (keep_1, send_1), (keep_2, send_2), third, parts[1:], width, ff
        )
        (d_outer,), (d_inner,) = d_outer, d_inner
        d_out, d_query, d_key, d_value = d_four
        token_grad = sum([g.astype(F32) for g in got], parts[0])
    return (
        layer_out.reshape(1, tok, width),
        token_grad.reshape(1, tok, width),
        d_query,
        vectors[0],
        d_key,
        d_value,
        vectors[1],
        d_out,
        vectors[2],
        vectors[3],
        vectors[4],
        d_inner,
        vectors[5],
        d_outer,
        vectors[6],
        vectors[7],
        vectors[8],
    )


def solution(mesh):
    token_spec = P("batch", "seq", None)
    placed = (token_spec, token_spec) + (P(),) * 15 + (P("batch"), P("batch", "seq", None, None))
    return jax.shard_map(
        on_device,
        mesh=mesh,
        in_specs=placed,
        out_specs=(token_spec, token_spec) + (P(),) * 15,
        check_vma=False,
    )
```
